32 devices in a mesh: ctx: 16 (over z, y, x), width: 2 (over core).
Axes of the slice: x: 2, y: 2, z: 4, core: 2. Of those that a mesh axis runs over, the one named last changes fastest.
Arguments:
- query_proj: bfloat16 [4096, 8192], P('ctx', 'width'), may hold values from -6 to 6
- key_proj: bfloat16 [4096, 8192], P('ctx', 'width'), may hold values from -6 to 6
- value_proj: bfloat16 [4096, 8192], P('ctx', 'width'), may hold values from -6 to 6
- short_kernel: float32 [3, 3, 8192], P(None, None, 'width'), may hold values from -3 to 3
- explicit_taps: bfloat16 [64, 512], P('width'), may hold values from -0.25 to 0.25
- decay_rate: float32 [64, 16], P('width'), may hold values from 0 to 1, as said below
- residues: float32 [64, 16], P('width'), may hold values from -3 to 3
- residual: bfloat16 [4096, 8192], P('ctx', 'width')
- norm_gain: float32 [8192], P('width'), may hold values from 0.5 to 1.5
Outputs:
- block_out: bfloat16 [4096, 8192], P('ctx', 'width')
- normed: bfloat16 [4096, 8192], P('ctx', 'width')
The draws below stay inside these ranges and needn't reach their ends.
Inputs may be any that keep to these rules, and one draw needn't show every extreme that they name: `decay_rate`: every decay rate is positive.
All inputs are finite; a program needn't handle non-finite values.
Results may differ from the reference program's by a relative error of at most 0.008.
Values may be sent and summed in bfloat16 or wider, within the bound.
No kernel may reach another device: no remote copies, remote signals or barrier semaphores. Data moves between devices by JAX's collectives and lax.ppermute only.
A program may use at most 128 MiB of HBM per device.

```python
import math
import jax
import jax.numpy as jnp
from jax import lax

D = 8192
MODES = 16
NG = 64
TAPS = 512
SEQ = 4096


def draw_decay_rate(key, part):
    jitter_key = jax.random.fold_in(key, 0)
    lowest = math.log(0.2 / SEQ)
    highest = math.log(1.0 / 30.0)
    jitter = jax.random.uniform(jitter_key, (NG, MODES))
    strata = (jnp.arange(MODES).astype(jnp.float32)[None, :] + jitter) / MODES
    return jnp.exp(lowest + strata * (highest - lowest)).astype(jnp.float32)


def draw_residues(key, part):
    sign_key, size_key = jax.random.split(key)
    signs = jnp.where(jax.random.bernoulli(sign_key, 0.5, (NG, MODES)), 1.0, -1.0)
    magnitude = jax.random.uniform(size_key, (NG, MODES), minval=0.5, maxval=1.0)
    rising = jnp.power(10.0, jnp.arange(NG).astype(jnp.float32) / NG - 0.6)[:, None]
    return (signs * magnitude * rising).astype(jnp.float32)


def draw_residual(key, part):
    base_key, column_key, row_key = jax.random.split(key, 3)
    columns = jnp.arange(D).astype(jnp.float32) / D
    column_scale = 0.1 * jnp.power(10.0, columns + jax.random.uniform(column_key, (D,), minval=-0.1, maxval=0.1))
    row_scale = jnp.power(10.0, jax.random.uniform(row_key, (SEQ, 1), minval=-0.5, maxval=0.5))
    values = jax.random.normal(base_key, (SEQ, D))
    return (values * row_scale * column_scale[None, :]).astype(jnp.bfloat16)


def block_levels(key, extent, cuts, least, high):
    def one(position, parts):
        steps = jax.random.uniform(jax.random.fold_in(jax.random.fold_in(key, 6), position), (parts,), jnp.float32, least / len(cuts), high / len(cuts))
        return jnp.repeat(jnp.exp(steps), extent[position] // parts).reshape((-1,) + (1,) * (len(extent) - position - 1))

    loudness = one(*cuts[0])
    for cut in cuts[1:]:
        loudness = loudness * one(*cut)
    return loudness


def centred(own_key, shape, scale, limit, pieces=(), kind=jnp.bfloat16):
    entries = jax.random.normal(own_key, shape, jnp.float32) * scale
    if len(pieces) > 0:
        entries = block_levels(own_key, shape, pieces, -0.22, 0.18) * entries
    return jnp.clip(entries, min=-limit, max=limit).astype(kind)


def setup_inputs(seed: int = 0) -> dict:
    key_of = jax.random.split(jax.random.key(seed), 10)
    return {
        "query_proj": centred(key_of[0], (SEQ, D), 1.0, 6.0, ((0, 16), (1, 2))),
        "key_proj": centred(key_of[1], (SEQ, D), 1.0, 6.0, ((0, 16), (1, 2))),
        "value_proj": centred(key_of[2], (SEQ, D), 1.0, 6.0, ((0, 16), (1, 2))),
        "short_kernel": centred(key_of[3], (3, 3, D), 0.6, 3.0, ((2, 2),), jnp.float32),
        "explicit_taps": centred(key_of[4], (NG, TAPS), TAPS ** -0.5, 0.25, ((0, 2),)),
        "decay_rate": draw_decay_rate(jax.random.fold_in(key_of[9], 71), 0),
        "residues": draw_residues(jax.random.fold_in(key_of[9], 71), 0),
        "residual": draw_residual(jax.random.fold_in(key_of[9], 71), 0),
        "norm_gain": jnp.clip(1.0 + 0.1 * jax.random.normal(key_of[8], (D,), jnp.float32), 0.5, 1.5),
    }


def shorten(rows, kern):
    values = rows.astype(jnp.float32)
    padded = jnp.pad(values, ((2, 0), (0, 0)))
    return kern[0] * values + kern[1] * padded[1:-1] + kern[2] * padded[:-2]

def reference(query_proj, key_proj, value_proj, short_kernel, explicit_taps, decay_rate, residues, residual, norm_gain):
    query_f = shorten(query_proj, short_kernel[0])
    key_f = shorten(key_proj, short_kernel[1])
    value_f = shorten(value_proj, short_kernel[2])
    mixer_input = (key_f * value_f).astype(jnp.bfloat16)
    group_count = decay_rate.shape[0]
    length = query_proj.shape[0]
    channels = query_proj.shape[1]
    group_size = channels // group_count
    weight = residues * jnp.sqrt(-jnp.expm1(-2.0 * decay_rate))
    lag_index = jnp.arange(length).astype(jnp.float32)
    explicit = jnp.pad(explicit_taps.astype(jnp.float32), ((0, 0), (0, length - explicit_taps.shape[1])))
    grouped = jnp.transpose(mixer_input.astype(jnp.float32).reshape(length, group_count, group_size), (1, 0, 2))

    def one_group(group_args):
        source, rate_row, weight_row, explicit_row = group_args
        modal_part = lax.optimization_barrier(jnp.sum(weight_row[:, None] * jnp.exp(-rate_row[:, None] * lag_index[None, :]), axis=0))
        filt = explicit_row + modal_part
        fft_len = 2 * length
        spectrum = jnp.fft.rfft(filt, n=fft_len)[:, None] * jnp.fft.rfft(source, n=fft_len, axis=0)
        return jnp.fft.irfft(spectrum, n=fft_len, axis=0)[:length].astype(jnp.float32)
    filtered = lax.map(one_group, (grouped, decay_rate, weight, explicit))
    filtered = jnp.transpose(filtered, (1, 0, 2)).reshape(length, channels)
    block_out = (residual.astype(jnp.float32) + query_f * filtered).astype(jnp.bfloat16)
    values = block_out.astype(jnp.float32)
    mean_sq = lax.optimization_barrier(jnp.mean(values * values, axis=1, keepdims=True))
    normed = (values * lax.rsqrt(mean_sq + 1e-05) * norm_gain).astype(jnp.bfloat16)
    return (block_out, normed)
```

```python
import jax
import jax.numpy as jnp
from jax import lax
from jax.experimental import pallas as pl
from jax.experimental.pallas import tpu as pltpu
from jax.sharding import PartitionSpec as P

F32 = jnp.float32
BF16 = jnp.bfloat16
LANES = 128


def shifted_pairs(length, by):
    return [(i, i + by) for i in range(length) if i + by < length]


def swap_pairs(length):
    return [(i, i ^ 1) for i in range(length)]


def dot(a, b):
    return jnp.dot(a, b, preferred_element_type=F32)


def split(x):
    hi = x.astype(BF16)
    return hi, (x - hi.astype(F32)).astype(BF16)


def short_filter(ref, tail, kern, lanes):
    rows = ref[:, lanes].astype(F32)
    return (
        kern[0] * rows
        + kern[1] * pltpu.roll(rows, 1, 0)
        + kern[2] * pltpu.roll(rows, 2, 0)
    )


def short_filter_top(ref, tail, kern, lanes):
    rows = ref[0:16, lanes].astype(F32)
    before, last = tail
    place = lax.broadcasted_iota(jnp.int32, rows.shape, 0)
    one = jnp.where(place == 0, last, pltpu.roll(rows, 1, 0))
    two = jnp.where(place == 0, before, jnp.where(place == 1, last, pltpu.roll(rows, 2, 0)))
    return kern[0] * rows + kern[1] * one + kern[2] * two


def mix_kernel(groups, k_ref, v_ref, tail_ref, sk_ref, rate_ref, x_ref, f_ref):
    length = k_ref.shape[0]
    for g in range(groups):
        lanes = slice(g * LANES, (g + 1) * LANES)
        k_kern = [sk_ref[1, j : j + 1, lanes] for j in range(3)]
        v_kern = [sk_ref[2, j : j + 1, lanes] for j in range(3)]
        k_tail = [tail_ref[j : j + 1, lanes] for j in (2, 3)]
        v_tail = [tail_ref[j : j + 1, lanes] for j in (4, 5)]
        x_ref[:, lanes] = (
            short_filter(k_ref, k_tail, k_kern, lanes) * short_filter(v_ref, v_tail, v_kern, lanes)
        ).astype(BF16)
        x_ref[0:16, lanes] = (
            short_filter_top(k_ref, k_tail, k_kern, lanes)
            * short_filter_top(v_ref, v_tail, v_kern, lanes)
        ).astype(BF16)
        rate = rate_ref[:, lanes]
        total = None
        for part in range(length // LANES):
            place = lax.broadcasted_iota(jnp.int32, rate.shape, 1) + part * LANES
            hi, lo = split(jnp.exp(-rate * (length - 1 - place).astype(F32)))
            data = x_ref[part * LANES : (part + 1) * LANES, lanes]
            term = dot(jnp.concatenate([hi, lo], axis=0), data)
            total = term if total is None else total + term
        modes = rate.shape[0]
        f_ref[:, lanes] = total[:modes] + total[modes:]


def table_kernel(
    groups, first_blocks, source_ref, rate_ref, weight_ref, xa_ref, xb_ref, tb_ref, fa_ref, fb_ref
):
    length = xa_ref.shape[0]
    width = source_ref.shape[-1]
    taps = width - LANES
    for g in range(groups):
        lanes = slice(g * LANES, (g + 1) * LANES)
        row = jnp.broadcast_to(source_ref[0, g : g + 1, :], (LANES, width))
        band = pltpu.roll(row, 0, 1, stride=1, stride_axis=0)
        tb_ref[g] = band[:, :taps].astype(BF16)
        rate = rate_ref[:, lanes]
        weight = weight_ref[:, lanes]
        pieces = []
        for part in range(3):
            place = lax.broadcasted_iota(jnp.int32, rate.shape, 1) + part * LANES
            lag = jnp.where(place <= LANES, LANES - place, 4 * LANES - place)
            inside = (place <= LANES) | (place > 2 * LANES)
            value = weight * jnp.exp(-rate * jnp.maximum(lag, 0).astype(F32))
            pieces.append(jnp.sum(jnp.where(inside, value, 0.0), axis=0, keepdims=True))
        modal = jnp.broadcast_to(jnp.concatenate(pieces, axis=1), (LANES, 3 * LANES))
        modal = pltpu.roll(modal, 0, 1, stride=1, stride_axis=0)
        near = band[:, taps - LANES :] + modal[:, : 2 * LANES]
        hi, lo = split(near)

        def apply(x_ref, out_ref):
            top = x_ref[0:LANES, lanes]
            both = x_ref[:, lanes]
            out_ref[0:LANES, lanes] = dot(hi[:, LANES:], top) + dot(lo[:, LANES:], top)
            out_ref[LANES:, lanes] = dot(hi, both) + dot(lo, both)

        @pl.when(pl.program_id(0) < first_blocks)
        def _():
            apply(xa_ref, fa_ref)

        @pl.when(pl.program_id(0) >= first_blocks)
        def _():
            apply(xb_ref, fb_ref)


def lag_one(tb, x):
    top = dot(tb[:, 256:512], x)
    low = dot(tb[:, 128:384], x)
    return top, low


def lag_two(tb, x):
    top = dot(tb[:, 0:256], x)
    low = dot(tb[:, 0:128], x[128:])
    return top, low


def merge_kernel(groups, odd_ref, tb_ref, near_ref, own_ref, fa_ref, send_ref, keep_ref):
    odd = odd_ref[0]

    @pl.when(odd == 1)
    def _():
        send_ref[...] = own_ref[...]
        for g in range(groups):
            lanes = slice(g * LANES, (g + 1) * LANES)
            top, low = lag_one(tb_ref[g], near_ref[:, lanes])
            keep_ref[0:LANES, lanes] = fa_ref[0:LANES, lanes] + top
            keep_ref[LANES:, lanes] = fa_ref[LANES:, lanes] + low

    @pl.when(odd == 0)
    def _():
        keep_ref[...] = fa_ref[...]
        for g in range(groups):
            lanes = slice(g * LANES, (g + 1) * LANES)
            top, low = lag_one(tb_ref[g], near_ref[:, lanes])
            top2, low2 = lag_two(tb_ref[g], own_ref[:, lanes])
            send_ref[0:LANES, lanes] = (top + top2).astype(BF16)
            send_ref[LANES:, lanes] = (low + low2).astype(BF16)


def late_kernel(
    groups,
    first_blocks,
    odd_ref,
    tb_ref,
    keep_ref,
    fb_ref,
    got_ref,
    near_ref,
    far_ref,
    state_ref,
    rate_ref,
    weight_ref,
    q_ref,
    tail_ref,
    sk_ref,
    residual_ref,
    out_ref,
    square_ref,
    acc_ref,
):
    odd = odd_ref[0]
    step = pl.program_id(0)
    length = q_ref.shape[0]

    @pl.when(step == 0)
    def _():
        square_ref[...] = jnp.zeros_like(square_ref)

    for g in range(groups):
        lanes = slice(g * LANES, (g + 1) * LANES)
        tb = tb_ref[g]
        rate = rate_ref[:, lanes]
        weight = weight_ref[:, lanes]
        s_hi, s_lo = split(state_ref[:, lanes])
        state = jnp.concatenate([s_hi, s_lo, s_hi], axis=0)
        for part in range(length // LANES):
            place = lax.broadcasted_iota(jnp.int32, rate.shape, 1) + part * LANES
            o_hi, o_lo = split(weight * jnp.exp(-rate * (place + 1).astype(F32)))
            table = jnp.concatenate([o_hi, o_hi, o_lo], axis=0)
            acc_ref[part * LANES : (part + 1) * LANES, :] = lax.dot_general(
                table, state, (((0,), (0,)), ((), ())), preferred_element_type=F32
            )

        @pl.when((step < first_blocks) & (odd == 1))
        def _():
            top, low = lag_two(tb, got_ref[:, lanes])
            acc_ref[0:LANES] += keep_ref[0:LANES, lanes] + top
            acc_ref[LANES:] += keep_ref[LANES:, lanes] + low

        @pl.when((step < first_blocks) & (odd == 0))
        def _():
            acc_ref[...] += keep_ref[:, lanes] + got_ref[:, lanes].astype(F32)

        @pl.when(step >= first_blocks)
        def _():
            top, low = lag_one(tb, near_ref[:, lanes])
            top2, low2 = lag_two(tb, far_ref[:, lanes])
            acc_ref[0:LANES] += fb_ref[0:LANES, lanes] + top + top2
            acc_ref[LANES:] += fb_ref[LANES:, lanes] + low + low2

        q_kern = [sk_ref[0, j : j + 1, lanes] for j in range(3)]
        tails = [tail_ref[j : j + 1, lanes] for j in (0, 1)]
        query = short_filter(q_ref, tails, q_kern, lanes)
        out = residual_ref[:, lanes].astype(F32) + query * acc_ref[...]
        out_ref[:, lanes] = out.astype(BF16)
        query_top = short_filter_top(q_ref, tails, q_kern, lanes)
        out_top = residual_ref[0:16, lanes].astype(F32) + query_top * acc_ref[0:16]
        out_ref[0:16, lanes] = out_top.astype(BF16)
        rounded = out_ref[:, lanes].astype(F32)
        square_ref[...] += rounded * rounded


def norm_kernel(scale_ref, gain_ref, x_ref, o_ref):
    o_ref[...] = (x_ref[...].astype(F32) * scale_ref[...] * gain_ref[...]).astype(BF16)


def cost(flops, moved):
    return pl.CostEstimate(flops=int(flops), bytes_accessed=int(moved), transcendentals=0)


def body(
    query_proj,
    key_proj,
    value_proj,
    short_kernel,
    explicit_taps,
    decay_rate,
    residues,
    residual,
    norm_gain,
):
    length, channels = query_proj.shape
    group_count, taps = explicit_taps.shape
    modes = decay_rate.shape[1]
    devices = lax.axis_size("ctx")
    per = max(group_count // 8, 1)
    steps = group_count // per
    first = (steps * 3) // 8
    second = steps - first
    lanes = per * LANES
    wide_a = first * lanes
    wide_b = second * lanes
    odd = (lax.axis_index("ctx") % 2).astype(jnp.int32).reshape(1)

    own_tail = jnp.concatenate(
        [query_proj[length - 2 :], key_proj[length - 2 :], value_proj[length - 2 :]], axis=0
    )
    tail = lax.ppermute(own_tail, "ctx", shifted_pairs(devices, 1)).astype(F32)

    weight = residues * jnp.sqrt(-jnp.expm1(-2.0 * decay_rate))
    spread = lambda t: jnp.repeat(t.T, LANES, axis=1)
    rate_c = spread(decay_rate)
    weight_c = spread(weight)
    source = jnp.pad(jnp.flip(explicit_taps, axis=1).astype(F32), ((0, 0), (1, LANES - 1)))
    source = source.reshape(steps, per, taps + LANES)

    smem = pl.BlockSpec(memory_space=pltpu.SMEM)

    def mix(offset, count):
        return pl.pallas_call(
            lambda *refs: mix_kernel(per, *refs),
            grid=(count,),
            in_specs=[
                pl.BlockSpec((length, lanes), lambda s: (0, s + offset)),
                pl.BlockSpec((length, lanes), lambda s: (0, s + offset)),
                pl.BlockSpec((6, lanes), lambda s: (0, s + offset)),
                pl.BlockSpec((3, 3, lanes), lambda s: (0, 0, s + offset)),
                pl.BlockSpec((modes, lanes), lambda s: (0, s + offset)),
            ],
            out_specs=[
                pl.BlockSpec((length, lanes), lambda s: (0, s)),
                pl.BlockSpec((modes, lanes), lambda s: (0, s)),
            ],
            out_shape=[
                jax.ShapeDtypeStruct((length, count * lanes), BF16),
                jax.ShapeDtypeStruct((modes, count * lanes), F32),
            ],
            cost_estimate=cost(0, count * lanes * length * 6),
            name="mix",
        )(key_proj, value_proj, tail, short_kernel, rate_c)

    xb, sum_b = mix(first, second)
    far = lax.ppermute(xb, "ctx", shifted_pairs(devices, 2))
    xa, sum_a = mix(0, first)
    near_a = lax.ppermute(xa, "ctx", swap_pairs(devices))

    window = jnp.concatenate([sum_a, sum_b], axis=1)
    state = jnp.zeros_like(window)
    hop = 1
    while hop < devices:
        got = lax.ppermute(window, "ctx", shifted_pairs(devices, hop))
        state = state + jnp.exp(-rate_c * (length * (hop - 1))) * got
        window = window + jnp.exp(-rate_c * (length * hop)) * got
        hop *= 2

    clamp_a = lambda s: (0, jnp.minimum(s, first - 1))
    clamp_b = lambda s: (0, jnp.maximum(s - first, 0))
    block_a = pl.BlockSpec((length, lanes), clamp_a)
    block_b = pl.BlockSpec((length, lanes), clamp_b)
    block = pl.BlockSpec((length, lanes), lambda s: (0, s))
    mode_block = pl.BlockSpec((modes, lanes), lambda s: (0, s))
    tb_block = pl.BlockSpec((per, LANES, taps), lambda s: (s, 0, 0))

    table, part_a, part_b = pl.pallas_call(
        lambda *refs: table_kernel(per, first, *refs),
        grid=(steps,),
        in_specs=[
            pl.BlockSpec((1, per, taps + LANES), lambda s: (s, 0, 0)),
            mode_block,
            mode_block,
            block_a,
            block_b,
        ],
        out_specs=[tb_block, block_a, block_b],
        out_shape=[
            jax.ShapeDtypeStruct((group_count, LANES, taps), BF16),
            jax.ShapeDtypeStruct((length, wide_a), F32),
            jax.ShapeDtypeStruct((length, wide_b), F32),
        ],
        cost_estimate=cost(0, 40e6),
        name="table",
    )(source, rate_c, weight_c, xa, xb)

    send_a, keep_a = pl.pallas_call(
        lambda *refs: merge_kernel(per, *refs),
        grid=(first,),
        in_specs=[smem, tb_block, block, block, block],
        out_specs=[block, block],
        out_shape=[
            jax.ShapeDtypeStruct((length, wide_a), BF16),
            jax.ShapeDtypeStruct((length, wide_a), F32),
        ],
        cost_estimate=cost(0, 8e6),
        name="merge",
    )(odd, table, near_a, xa, part_a)
    got_a = lax.ppermute(send_a, "ctx", shifted_pairs(devices, 2))

    send_b = jnp.where(odd[0] == 1, far, xb)
    near_b = lax.ppermute(send_b, "ctx", swap_pairs(devices))

    block_out, squares = pl.pallas_call(
        lambda *refs: late_kernel(per, first, *refs),
        grid=(steps,),
        in_specs=[
            smem,
            tb_block,
            block_a,
            block_b,
            block_a,
            block_b,
            block_b,
            mode_block,
            mode_block,
            mode_block,
            block,
            pl.BlockSpec((6, lanes), lambda s: (0, s)),
            pl.BlockSpec((3, 3, lanes), lambda s: (0, 0, s)),
            block,
        ],
        out_specs=[block, pl.BlockSpec((length, LANES), lambda s: (0, 0))],
        out_shape=[
            jax.ShapeDtypeStruct((length, channels), BF16),
            jax.ShapeDtypeStruct((length, LANES), F32),
        ],
        scratch_shapes=[pltpu.VMEM((length, LANES), F32)],
        cost_estimate=cost(0, 20e6),
        name="late",
    )(
        odd,
        table,
        keep_a,
        part_b,
        got_a,
        near_b,
        far,
        state,
        rate_c,
        weight_c,
        query_proj,
        tail,
        short_kernel,
        residual,
    )
    total = lax.psum(jnp.sum(squares, axis=1), "width")
    mean_sq = total / (channels * lax.axis_size("width"))
    scale = lax.rsqrt(mean_sq + 1e-05)[:, None]
    normed = pl.pallas_call(
        norm_kernel,
        grid=(steps,),
        in_specs=[
            pl.BlockSpec((length, 1), lambda s: (0, 0)),
            pl.BlockSpec((1, lanes), lambda s: (0, s)),
            block,
        ],
        out_specs=block,
        out_shape=jax.ShapeDtypeStruct((length, channels), BF16),
        cost_estimate=cost(0, 4e6),
        name="norm",
    )(scale, norm_gain[None, :], block_out)
    return (block_out, normed)


def solution(mesh):
    return jax.shard_map(
        body,
        mesh=mesh,
        in_specs=(
            P("ctx", "width"),
            P("ctx", "width"),
            P("ctx", "width"),
            P(None, None, "width"),
            P("width", None),
            P("width", None),
            P("width", None),
            P("ctx", "width"),
            P("width"),
        ),
        out_specs=(P("ctx", "width"), P("ctx", "width")),
        check_vma=False,
    )
```

```python
import jax
import jax.numpy as jnp
from jax import lax
from jax.experimental import pallas as pl
from jax.experimental.pallas import tpu as pltpu
from jax.sharding import PartitionSpec as P

F32 = jnp.float32
BF16 = jnp.bfloat16
LANES = 128


def shifted_pairs(length, by):
    return [(i, i + by) for i in range(length) if i + by < length]


def swap_pairs(length):
    return [(i, i ^ 1) for i in range(length)]


def dot(a, b):
    return jnp.dot(a, b, preferred_element_type=F32)


def split(x):
    hi = x.astype(BF16)
    return hi, (x - hi.astype(F32)).astype(BF16)


def each(count, body, unroll):
    def several(step, carry):
        for j in range(unroll):
            body(step * unroll + j)
        return carry

    lax.fori_loop(0, count // unroll, several, 0)
    for group in range(count - count % unroll, count):
        body(group)


def after(value, *others):
    return lax.optimization_barrier((value, *others))[0]


def at(group):
    if isinstance(group, int):
        return pl.ds(group * LANES, LANES)
    return pl.ds(pl.multiple_of(group * LANES, LANES), LANES)


def column(table, group):
    place = lax.broadcasted_iota(jnp.int32, table.shape, 1)
    picked = jnp.sum(jnp.where(place == group, table, 0.0), axis=1, keepdims=True)
    return jnp.broadcast_to(picked, (table.shape[0], LANES))


def taps_of(sk_ref, which, lanes):
    return [sk_ref[which, j : j + 1, lanes] for j in range(3)]


def tails_of(tail_ref, which, lanes):
    rows = tail_ref[0:8, lanes].astype(F32)
    return [rows[2 * which + j : 2 * which + j + 1] for j in range(2)]


def short_filter(ref, kern, lanes):
    rows = ref[:, lanes].astype(F32)
    return kern[0] * rows + kern[1] * pltpu.roll(rows, 1, 0) + kern[2] * pltpu.roll(rows, 2, 0)


def short_filter_top(ref, tail, kern, lanes):
    rows = ref[0:16, lanes].astype(F32)
    before, last = tail
    place = lax.broadcasted_iota(jnp.int32, rows.shape, 0)
    one = jnp.where(place == 0, last, pltpu.roll(rows, 1, 0))
    two = jnp.where(place == 0, before, jnp.where(place == 1, last, pltpu.roll(rows, 2, 0)))
    return kern[0] * rows + kern[1] * one + kern[2] * two


def tail_kernel(q_ref, k_ref, v_ref, o_ref):
    for which, ref in enumerate((q_ref, k_ref, v_ref)):
        o_ref[2 * which : 2 * which + 2, :] = ref[14:16, :]
    o_ref[6:8, :] = v_ref[14:16, :]


def mix_kernel(sizes, k_ref, v_ref, sk_ref, *x_refs):
    def make(start, x_ref):
        def one(g):
            source = at(g + start)
            x_ref[:, at(g)] = (
                short_filter(k_ref, taps_of(sk_ref, 1, source), source)
                * short_filter(v_ref, taps_of(sk_ref, 2, source), source)
            ).astype(BF16)

        return one

    start = 0
    for size, x_ref in zip(sizes, x_refs):
        each(size, make(start, x_ref), 2)
        start += size


def head_kernel(sizes, *refs):
    k_ref, v_ref, tail_ref, sk_ref, rate_ref, *x_refs, f_ref = refs[len(sizes) :]
    length = k_ref.shape[0]

    def make(start, x_ref):
        def one(g):
            source = at(g + start)
            lanes = at(g)
            x_ref[0:16, lanes] = (
                short_filter_top(
                    k_ref, tails_of(tail_ref, 1, source), taps_of(sk_ref, 1, source), source
                )
                * short_filter_top(
                    v_ref, tails_of(tail_ref, 2, source), taps_of(sk_ref, 2, source), source
                )
            ).astype(BF16)
            rate = column(rate_ref[...], g + start)
            tables = []
            for part in range(length // LANES):
                place = lax.broadcasted_iota(jnp.int32, rate.shape, 1) + part * LANES
                tables.append(jnp.exp(-rate * (length - 1 - place).astype(F32)))
            hi, lo = split(jnp.concatenate(tables, axis=1))
            total = dot(jnp.concatenate([hi, lo], axis=0), x_ref[:, lanes])
            modes = rate.shape[0]
            f_ref[:, source] = total[:modes] + total[modes:]

        return one

    start = 0
    for size, x_ref in zip(sizes, x_refs):
        each(size, make(start, x_ref), 2)
        start += size


def table_kernel(start, pieces, source_ref, rate_ref, weight_ref, *refs):
    *x_refs, tb_ref, f_ref = refs
    done = 0
    for groups, x_ref in zip(pieces, x_refs):
        table_piece(start, done, groups, source_ref, rate_ref, weight_ref, x_ref, tb_ref, f_ref)
        done += groups


def table_piece(start, skip, groups, source_ref, rate_ref, weight_ref, x_ref, tb_ref, f_ref):
    taps = source_ref.shape[-1]
    row_at = lax.broadcasted_iota(jnp.int32, (LANES, LANES), 0)
    col_at = lax.broadcasted_iota(jnp.int32, (LANES, LANES), 1)
    below = col_at <= row_at
    place = lax.broadcasted_iota(jnp.int32, (1, LANES), 1)

    def one(g):
        lanes = at(g)
        taken = source_ref[pl.ds(g + start + skip, 1), :]
        band = pltpu.roll(jnp.broadcast_to(taken, (LANES, taps)), 0, 1, stride=1, stride_axis=0)
        tb_ref[g + skip, :, 0:LANES] = jnp.where(below, 0.0, band[:, 0:LANES]).astype(BF16)
        tb_ref[g + skip, :, LANES:] = band[:, LANES:].astype(BF16)
        rate = column(rate_ref[...], g + start + skip)
        weight = column(weight_ref[...], g + start + skip)

        def modal(lag):
            value = weight * jnp.exp(-rate * lag.astype(F32))
            return jnp.sum(value, axis=0, keepdims=True)

        first = taken[:, taps - LANES :] + modal(LANES - place)
        lag_zero = taken[:, 0:1] + modal(place * 0)[:, 0:1]
        second = taken[:, taps - 2 * LANES : taps - LANES] + modal(2 * LANES - place)
        second = jnp.where(place == 0, lag_zero, second)
        near = jnp.broadcast_to(jnp.concatenate([first, second], axis=1), (LANES, 2 * LANES))
        near = pltpu.roll(near, 0, 1, stride=1, stride_axis=0)
        zero_lag = jnp.where(below, near[:, LANES:], 0.0)
        low = jnp.concatenate([near[:, :LANES], zero_lag], axis=1)
        top = jnp.concatenate([zero_lag, jnp.zeros((LANES, LANES), F32)], axis=1)
        hi, lo = split(jnp.concatenate([top, low], axis=0))
        both = dot(jnp.concatenate([hi, lo], axis=0), x_ref[:, lanes])
        f_ref[:, at(g + skip)] = both[: 2 * LANES] + both[2 * LANES :]

    each(groups, one, 2)


def lag_one(tb_ref, g):
    return jnp.concatenate([tb_ref[g, :, 256:512], tb_ref[g, :, 128:384]], axis=0)


def lag_two(tb_ref, g):
    low = jnp.concatenate([jnp.zeros((LANES, LANES), BF16), tb_ref[g, :, 0:128]], axis=1)
    return jnp.concatenate([tb_ref[g, :, 0:256], low], axis=0)


def merge_kernel(
    first,
    b_parts,
    odd_ref,
    tb_ref,
    near_ref,
    own_ref,
    f_ref,
    far1_ref,
    far2_ref,
    xb1_ref,
    xb2_ref,
    send_a_ref,
    send_b_ref,
    keep_ref,
):
    odd = odd_ref[0]
    middle = b_parts[0] * LANES

    @pl.when(odd == 1)
    def _():
        send_a_ref[...] = own_ref[...]
        send_b_ref[:, :middle] = far1_ref[...]
        send_b_ref[:, middle:] = far2_ref[...]

        def one(g):
            lanes = at(g)
            keep_ref[:, lanes] = f_ref[:, lanes] + dot(lag_one(tb_ref, g), near_ref[:, lanes])

        each(first, one, 2)

    @pl.when(odd == 0)
    def _():
        keep_ref[...] = f_ref[...]
        send_b_ref[:, :middle] = xb1_ref[...]
        send_b_ref[:, middle:] = xb2_ref[...]

        def one(g):
            lanes = at(g)
            send_a_ref[:, lanes] = (
                dot(lag_one(tb_ref, g), near_ref[:, lanes])
                + dot(lag_two(tb_ref, g), own_ref[:, lanes])
            ).astype(BF16)

        each(first, one, 2)


def pre_kernel(
    start, one, two, tb_ref, far1_ref, far2_ref, f_ref, q_ref, tail_ref, sk_ref, acc_ref, query_ref
):
    def filtered(g):
        lanes = at(g)
        kern = taps_of(sk_ref, 0, lanes)
        query_ref[:, lanes] = short_filter(q_ref, kern, lanes)
        query_ref[0:16, lanes] = short_filter_top(q_ref, tails_of(tail_ref, 0, lanes), kern, lanes)

    each(start, filtered, 2)

    def make(skip, far_ref):
        def added(g):
            lanes = at(g + skip)
            filtered(g + skip + start)
            acc_ref[:, lanes] = f_ref[:, lanes] + dot(lag_two(tb_ref, g + skip), far_ref[:, at(g)])

        return added

    each(one, make(0, far1_ref), 2)
    each(two, make(one, far2_ref), 2)


def state_kernel(
    first, second, fa_ref, fb_ref, state_ref, rate_ref, weight_ref, query_ref, res_ref, base_ref
):
    length = fa_ref.shape[0]

    def make(start, ref):
        def one(g):
            lanes = at(g)
            wide = at(g + start)
            rate = column(rate_ref[...], g + start)
            weight = column(weight_ref[...], g + start)
            s_hi, s_lo = split(state_ref[:, wide])
            state = jnp.concatenate([s_hi, s_lo, s_hi], axis=0)
            tables = []
            for part in range(length // LANES):
                place = lax.broadcasted_iota(jnp.int32, rate.shape, 1) + part * LANES
                tables.append(weight * jnp.exp(-rate * (place + 1).astype(F32)))
            o_hi, o_lo = split(jnp.concatenate(tables, axis=1))
            table = jnp.concatenate([o_hi, o_hi, o_lo], axis=0)
            far = lax.dot_general(
                table, state, (((0,), (0,)), ((), ())), preferred_element_type=F32
            )
            base_ref[:, wide] = res_ref[:, wide].astype(F32) + query_ref[:, wide] * (
                ref[:, lanes] + far
            )

        return one

    each(first, make(0, fa_ref), 2)
    each(second, make(first, fb_ref), 2)


def chunks_of(groups):
    return [(c * groups // 8, (c + 1) * groups // 8) for c in range(8)]


def copy_out(source_ref, target_ref, sems, index, low, high):
    span = pl.ds(low * LANES, (high - low) * LANES)
    return pltpu.make_async_copy(source_ref.at[:, span], target_ref.at[:, span], sems.at[index])


def late_kernel(
    first,
    second,
    odd_ref,
    ta_ref,
    tb_ref,
    got_ref,
    near_ref,
    base_ref,
    query_ref,
    target_ref,
    out_ref,
    square_ref,
    sum_ref,
    sems,
):
    odd = odd_ref[0]
    sum_ref[...] = jnp.zeros_like(sum_ref)

    def finish(wide, term):
        rounded = (base_ref[:, wide] + query_ref[:, wide] * term).astype(BF16)
        out_ref[:, wide] = rounded
        back = rounded.astype(F32)
        sum_ref[...] += back * back

    def far(g):
        finish(at(g), dot(lag_two(ta_ref, g), got_ref[:, at(g)]))

    def merged(g):
        finish(at(g), got_ref[:, at(g)].astype(F32))

    def near(g):
        finish(at(g + first), dot(lag_one(tb_ref, g), near_ref[:, at(g)]))

    @pl.when(odd == 1)
    def _():
        each(first, far, 2)

    @pl.when(odd == 0)
    def _():
        each(first, merged, 2)

    copy_a = copy_out(out_ref, target_ref, sems, 0, 0, first)
    copy_a.start()
    each(second, near, 2)
    copy_b = copy_out(out_ref, target_ref, sems, 1, first, first + second)
    copy_b.start()
    turned = jnp.transpose(sum_ref[...])
    square_ref[...] = jnp.broadcast_to(jnp.sum(turned, axis=0, keepdims=True), square_ref.shape)
    copy_a.wait()
    copy_b.wait()


def norm_kernel(count, groups, total_ref, gain_ref, x_ref, target_ref, o_ref, sems):
    scale = jnp.transpose(lax.rsqrt(total_ref[...] * (1.0 / count) + 1e-05))
    wide = jnp.broadcast_to(scale[:, 0:1], (scale.shape[0], LANES))
    copies = []
    for index, (low, high) in enumerate(chunks_of(groups)):
        for g in range(low, high):
            lanes = at(g)
            o_ref[:, lanes] = (x_ref[:, lanes].astype(F32) * wide * gain_ref[:, lanes]).astype(BF16)
        copy = copy_out(o_ref, target_ref, sems, index, low, high)
        copy.start()
        copies.append(copy)
    for copy in copies:
        copy.wait()


def call(kernel, out_shape, name, *args, smem=0, scratch=(), loose=(), alias={}):
    specs = [pl.BlockSpec(memory_space=pltpu.SMEM)] * smem
    specs += [pl.BlockSpec(memory_space=pltpu.VMEM)] * (len(args) - smem)
    outs = [
        pl.BlockSpec(memory_space=pl.ANY if i in loose else pltpu.VMEM)
        for i in range(len(out_shape))
    ]
    return pl.pallas_call(
        kernel,
        in_specs=specs,
        out_specs=outs,
        out_shape=out_shape,
        scratch_shapes=scratch,
        input_output_aliases=alias,
        cost_estimate=pl.CostEstimate(flops=0, bytes_accessed=20000, transcendentals=0),
        compiler_params=pltpu.CompilerParams(vmem_limit_bytes=24 << 20),
        name=name,
    )(*args)


def body(
    query_proj,
    key_proj,
    value_proj,
    short_kernel,
    explicit_taps,
    decay_rate,
    residues,
    residual,
    norm_gain,
):
    length, channels = query_proj.shape
    groups, taps = explicit_taps.shape
    modes = decay_rate.shape[1]
    devices = lax.axis_size("ctx")
    first = groups // 2
    second = groups - first
    b_parts = ((second * 3) // 8, second - (second * 3) // 8)
    sizes = (first, *b_parts)
    wide_a = first * LANES
    wide_b = second * LANES
    odd = (lax.axis_index("ctx") % 2).astype(jnp.int32).reshape(1)
    is_odd = odd[0] == 1
    shape = jax.ShapeDtypeStruct

    last = pl.BlockSpec((16, channels), lambda s: (length // 16 - 1, 0))
    own_tail = pl.pallas_call(
        tail_kernel,
        grid=(1,),
        in_specs=[last, last, last],
        out_specs=pl.BlockSpec((8, channels), lambda s: (0, 0)),
        out_shape=shape((8, channels), BF16),
        name="tail",
    )(query_proj, key_proj, value_proj)
    tail = lax.ppermute(own_tail, "ctx", shifted_pairs(devices, 1))

    rate_t = decay_rate.T
    weight_t = (residues * jnp.sqrt(-jnp.expm1(-2.0 * decay_rate))).T
    flipped = jnp.flip(explicit_taps, axis=1).astype(F32)
    source = jnp.concatenate([flipped[:, taps - 1 :], flipped[:, : taps - 1]], axis=1)

    blocks = [shape((length, size * LANES), BF16) for size in sizes]
    mixed = call(
        lambda *refs: mix_kernel(sizes, *refs), blocks, "mix", key_proj, value_proj, short_kernel
    )
    xa, xb1, xb2, window = call(
        lambda *refs: head_kernel(sizes, *refs),
        [*blocks, shape((modes, channels), F32)],
        "head",
        *mixed, key_proj, value_proj, after(tail, mixed[0]), short_kernel, rate_t,
        alias={i: i for i in range(len(sizes))},
    )
    half = channels // 2
    mine = jnp.where(is_odd, window[:, half:], window[:, :half])
    beside = lax.ppermute(
        jnp.where(is_odd, window[:, :half], window[:, half:]), "ctx", swap_pairs(devices)
    )

    def tables(start, parts, x, source):
        count = sum(parts)
        return call(
            lambda *refs: table_kernel(start, parts, *refs),
            [shape((count, LANES, taps), BF16), shape((length, count * LANES), F32)],
            "table",
            source, rate_t, weight_t, *x,
        )

    wide_rate = jnp.broadcast_to(rate_t[:, :, None], (modes, groups, LANES)).reshape(modes, channels)
    wide_rate = jnp.where(is_odd, wide_rate[:, half:], wide_rate[:, :half])
    decay = lambda blocks: jnp.exp(-wide_rate * (length * blocks))

    ta, part_a = tables(0, (first,), (xa,), source)
    beside = after(beside, part_a)
    pair = decay(1.0) * jnp.where(is_odd, beside, mine) + jnp.where(is_odd, mine, beside)
    far1 = lax.ppermute(xb1, "ctx", shifted_pairs(devices, 2))
    near_a = lax.ppermute(xa, "ctx", swap_pairs(devices))
    got = lax.ppermute(pair, "ctx", shifted_pairs(devices, 2))
    tb, part_b = tables(first, b_parts, (xb1, xb2), after(source, pair))
    before = after(got, part_b)
    pair = pair + decay(2.0) * before
    far1 = after(far1, part_b)
    far2 = lax.ppermute(after(xb2, far1, pair), "ctx", shifted_pairs(devices, 2))
    near_a = after(near_a, part_b)
    hop = 4
    while hop < devices:
        got = lax.ppermute(pair, "ctx", shifted_pairs(devices, hop))
        before = before + decay(float(hop - 2)) * got
        pair = pair + decay(float(hop)) * got
        hop *= 2
        if hop * 2 == devices:
            far2, near_a = after(far2, pair), after(near_a, pair)
    send_a, send_b, keep_a = call(
        lambda *refs: merge_kernel(first, b_parts, *refs),
        [
            shape((length, wide_a), BF16),
            shape((length, wide_b), BF16),
            shape((length, wide_a), F32),
        ],
        "merge",
        odd, ta, near_a, xa, part_a, far1, far2, xb1, xb2,
        smem=1,
    )
    onward = decay(1.0) * before + jnp.where(is_odd, beside, mine)
    other = lax.ppermute(
        after(jnp.where(is_odd, before, onward), keep_a), "ctx", swap_pairs(devices)
    )
    near_b = lax.ppermute(after(send_b, onward), "ctx", swap_pairs(devices))
    got_a = lax.ppermute(send_a, "ctx", shifted_pairs(devices, 2))
    acc_b, query = call(
        lambda *refs: pre_kernel(first, *b_parts, *refs),
        [shape((length, wide_b), F32), shape((length, channels), F32)],
        "pre",
        tb, far1, far2, after(part_b, keep_a), query_proj, tail, short_kernel,
    )
    other = after(other, query)
    state = jnp.where(
        is_odd,
        jnp.concatenate([other, onward], axis=1),
        jnp.concatenate([before, other], axis=1),
    )
    (base,) = call(
        lambda *refs: state_kernel(first, second, *refs),
        [shape((length, channels), F32)],
        "state",
        keep_a, acc_b, state, rate_t, weight_t, query, residual,
    )
    block_out, again, squares = call(
        lambda *refs: late_kernel(first, second, *refs),
        [
            shape((length, channels), BF16),
            shape((length, channels), BF16),
            shape((8, length), F32),
        ],
        "late",
        odd, ta, tb, got_a, near_b, base, query,
        smem=1,
        scratch=[pltpu.VMEM((length, LANES), F32), pltpu.SemaphoreType.DMA((2,))],
        loose=(0,),
    )
    total = lax.psum(squares, "width")
    count = float(channels * lax.axis_size("width"))
    (normed,) = call(
        lambda *refs: norm_kernel(count, groups, *refs),
        [shape((length, channels), BF16)],
        "norm",
        total, norm_gain[None, :], again,
        scratch=[pltpu.VMEM((length, channels), BF16), pltpu.SemaphoreType.DMA((8,))],
        loose=(0,),
    )
    return (block_out, normed)


def solution(mesh):
    return jax.shard_map(
        body,
        mesh=mesh,
        in_specs=(
            P("ctx", "width"),
            P("ctx", "width"),
            P("ctx", "width"),
            P(None, None, "width"),
            P("width", None),
            P("width", None),
            P("width", None),
            P("ctx", "width"),
            P("width"),
        ),
        out_specs=(P("ctx", "width"), P("ctx", "width")),
        check_vma=False,
    )
```

```python
import jax
import jax.numpy as jnp
from jax import lax
from jax.experimental import pallas as pl
from jax.experimental.pallas import tpu as pltpu
from jax.sharding import PartitionSpec as P

F32 = jnp.float32
BF16 = jnp.bfloat16
LANES = 128


def shifted_pairs(length, by):
    return [(i, i + by) for i in range(length) if i + by < length]


def swap_pairs(length):
    return [(i, i ^ 1) for i in range(length)]


def dot(a, b):
    return jnp.dot(a, b, preferred_element_type=F32)


def split(x):
    hi = x.astype(BF16)
    return hi, (x - hi.astype(F32)).astype(BF16)


def each(count, body, unroll):
    def several(step, carry):
        for j in range(unroll):
            body(step * unroll + j)
        return carry

    lax.fori_loop(0, count // unroll, several, 0)
    for group in range(count - count % unroll, count):
        body(group)


def after(value, *others):
    return lax.optimization_barrier((value, *others))[0]


def at(group):
    if isinstance(group, int):
        return pl.ds(group * LANES, LANES)
    return pl.ds(pl.multiple_of(group * LANES, LANES), LANES)


def column(table, group):
    place = lax.broadcasted_iota(jnp.int32, table.shape, 1)
    picked = jnp.sum(jnp.where(place == group, table, 0.0), axis=1, keepdims=True)
    return jnp.broadcast_to(picked, (table.shape[0], LANES))


def taps_of(sk_ref, which, lanes):
    return [sk_ref[which, j : j + 1, lanes] for j in range(3)]


def tails_of(tail_ref, which, lanes):
    rows = tail_ref[0:8, lanes].astype(F32)
    return [rows[2 * which + j : 2 * which + j + 1] for j in range(2)]


def short_filter(ref, kern, lanes):
    rows = ref[:, lanes].astype(F32)
    return kern[0] * rows + kern[1] * pltpu.roll(rows, 1, 0) + kern[2] * pltpu.roll(rows, 2, 0)


def short_filter_top(ref, tail, kern, lanes):
    rows = ref[0:16, lanes].astype(F32)
    before, last = tail
    place = lax.broadcasted_iota(jnp.int32, rows.shape, 0)
    one = jnp.where(place == 0, last, pltpu.roll(rows, 1, 0))
    two = jnp.where(place == 0, before, jnp.where(place == 1, last, pltpu.roll(rows, 2, 0)))
    return kern[0] * rows + kern[1] * one + kern[2] * two


def tail_kernel(q_ref, k_ref, v_ref, o_ref):
    for which, ref in enumerate((q_ref, k_ref, v_ref)):
        o_ref[2 * which : 2 * which + 2, :] = ref[14:16, :]
    o_ref[6:8, :] = v_ref[14:16, :]


def mix_kernel(sizes, k_ref, v_ref, sk_ref, *x_refs):
    def make(start, x_ref):
        def one(g):
            source = at(g + start)
            x_ref[:, at(g)] = (
                short_filter(k_ref, taps_of(sk_ref, 1, source), source)
                * short_filter(v_ref, taps_of(sk_ref, 2, source), source)
            ).astype(BF16)

        return one

    start = 0
    for size, x_ref in zip(sizes, x_refs):
        each(size, make(start, x_ref), 2)
        start += size


def head_kernel(sizes, *refs):
    k_ref, v_ref, tail_ref, sk_ref, rate_ref, *x_refs, f_ref = refs[len(sizes) :]
    for source, x_ref in zip(refs, x_refs):
        x_ref[...] = source[...]
    length = k_ref.shape[0]

    def make(start, x_ref):
        def one(g):
            source = at(g + start)
            lanes = at(g)
            x_ref[0:16, lanes] = (
                short_filter_top(
                    k_ref, tails_of(tail_ref, 1, source), taps_of(sk_ref, 1, source), source
                )
                * short_filter_top(
                    v_ref, tails_of(tail_ref, 2, source), taps_of(sk_ref, 2, source), source
                )
            ).astype(BF16)
            rate = column(rate_ref[...], g + start)
            tables = []
            for part in range(length // LANES):
                place = lax.broadcasted_iota(jnp.int32, rate.shape, 1) + part * LANES
                tables.append(jnp.exp(-rate * (length - 1 - place).astype(F32)))
            hi, lo = split(jnp.concatenate(tables, axis=1))
            total = dot(jnp.concatenate([hi, lo], axis=0), x_ref[:, lanes])
            modes = rate.shape[0]
            f_ref[:, source] = total[:modes] + total[modes:]

        return one

    start = 0
    for size, x_ref in zip(sizes, x_refs):
        each(size, make(start, x_ref), 2)
        start += size


def table_kernel(start, pieces, source_ref, rate_ref, weight_ref, *refs):
    *x_refs, tb_ref, f_ref = refs
    done = 0
    for groups, x_ref in zip(pieces, x_refs):
        table_piece(start, done, groups, source_ref, rate_ref, weight_ref, x_ref, tb_ref, f_ref)
        done += groups


def table_piece(start, skip, groups, source_ref, rate_ref, weight_ref, x_ref, tb_ref, f_ref):
    taps = source_ref.shape[-1]
    row_at = lax.broadcasted_iota(jnp.int32, (LANES, LANES), 0)
    col_at = lax.broadcasted_iota(jnp.int32, (LANES, LANES), 1)
    below = col_at <= row_at
    place = lax.broadcasted_iota(jnp.int32, (1, LANES), 1)

    def one(g):
        lanes = at(g)
        taken = source_ref[pl.ds(g + start + skip, 1), :]
        band = pltpu.roll(jnp.broadcast_to(taken, (LANES, taps)), 0, 1, stride=1, stride_axis=0)
        tb_ref[g + skip, :, 0:LANES] = jnp.where(below, 0.0, band[:, 0:LANES]).astype(BF16)
        tb_ref[g + skip, :, LANES:] = band[:, LANES:].astype(BF16)
        rate = column(rate_ref[...], g + start + skip)
        weight = column(weight_ref[...], g + start + skip)

        def modal(lag):
            value = weight * jnp.exp(-rate * lag.astype(F32))
            return jnp.sum(value, axis=0, keepdims=True)

        first = taken[:, taps - LANES :] + modal(LANES - place)
        lag_zero = taken[:, 0:1] + modal(place * 0)[:, 0:1]
        second = taken[:, taps - 2 * LANES : taps - LANES] + modal(2 * LANES - place)
        second = jnp.where(place == 0, lag_zero, second)
        near = jnp.broadcast_to(jnp.concatenate([first, second], axis=1), (LANES, 2 * LANES))
        near = pltpu.roll(near, 0, 1, stride=1, stride_axis=0)
        zero_lag = jnp.where(below, near[:, LANES:], 0.0)
        low = jnp.concatenate([near[:, :LANES], zero_lag], axis=1)
        top = jnp.concatenate([zero_lag, jnp.zeros((LANES, LANES), F32)], axis=1)
        hi, lo = split(jnp.concatenate([top, low], axis=0))
        both = dot(jnp.concatenate([hi, lo], axis=0), x_ref[:, lanes])
        f_ref[:, at(g + skip)] = both[: 2 * LANES] + both[2 * LANES :]

    each(groups, one, 2)


def lag_one(tb_ref, g):
    return jnp.concatenate([tb_ref[g, :, 256:512], tb_ref[g, :, 128:384]], axis=0)


def lag_two(tb_ref, g):
    low = jnp.concatenate([jnp.zeros((LANES, LANES), BF16), tb_ref[g, :, 0:128]], axis=1)
    return jnp.concatenate([tb_ref[g, :, 0:256], low], axis=0)


def merge_kernel(
    a_parts,
    b_parts,
    odd_ref,
    tb_ref,
    near1_ref,
    near2_ref,
    own1_ref,
    own2_ref,
    f_ref,
    far1_ref,
    far2_ref,
    xb1_ref,
    xb2_ref,
    send_a_ref,
    send_b_ref,
    keep_ref,
):
    odd = odd_ref[0]
    edge = a_parts[0] * LANES
    middle = b_parts[0] * LANES

    @pl.when(odd == 1)
    def _():
        send_a_ref[:, :edge] = own1_ref[...]
        send_a_ref[:, edge:] = own2_ref[...]
        send_b_ref[:, :middle] = far1_ref[...]
        send_b_ref[:, middle:] = far2_ref[...]

        def make(skip, near_ref):
            def one(g):
                wide = at(g + skip)
                keep_ref[:, wide] = f_ref[:, wide] + dot(
                    lag_one(tb_ref, g + skip), near_ref[:, at(g)]
                )

            return one

        each(a_parts[0], make(0, near1_ref), 2)
        each(a_parts[1], make(a_parts[0], near2_ref), 2)

    @pl.when(odd == 0)
    def _():
        keep_ref[...] = f_ref[...]
        send_b_ref[:, :middle] = xb1_ref[...]
        send_b_ref[:, middle:] = xb2_ref[...]

        def make(skip, near_ref, own_ref):
            def one(g):
                send_a_ref[:, at(g + skip)] = (
                    dot(lag_one(tb_ref, g + skip), near_ref[:, at(g)])
                    + dot(lag_two(tb_ref, g + skip), own_ref[:, at(g)])
                ).astype(BF16)

            return one

        each(a_parts[0], make(0, near1_ref, own1_ref), 2)
        each(a_parts[1], make(a_parts[0], near2_ref, own2_ref), 2)


def pre_kernel(
    start, one, two, tb_ref, far1_ref, far2_ref, f_ref, q_ref, tail_ref, sk_ref, acc_ref, query_ref
):
    def filtered(g):
        lanes = at(g)
        kern = taps_of(sk_ref, 0, lanes)
        query_ref[:, lanes] = short_filter(q_ref, kern, lanes)
        query_ref[0:16, lanes] = short_filter_top(q_ref, tails_of(tail_ref, 0, lanes), kern, lanes)

    each(start, filtered, 2)

    def make(skip, far_ref):
        def added(g):
            lanes = at(g + skip)
            filtered(g + skip + start)
            acc_ref[:, lanes] = f_ref[:, lanes] + dot(lag_two(tb_ref, g + skip), far_ref[:, at(g)])

        return added

    each(one, make(0, far1_ref), 2)
    each(two, make(one, far2_ref), 2)


def state_kernel(
    first, second, fa_ref, fb_ref, state_ref, rate_ref, weight_ref, query_ref, res_ref, base_ref
):
    length = fa_ref.shape[0]

    def make(start, ref):
        def one(g):
            lanes = at(g)
            wide = at(g + start)
            rate = column(rate_ref[...], g + start)
            weight = column(weight_ref[...], g + start)
            s_hi, s_lo = split(state_ref[:, wide])
            state = jnp.concatenate([s_hi, s_lo, s_hi], axis=0)
            tables = []
            for part in range(length // LANES):
                place = lax.broadcasted_iota(jnp.int32, rate.shape, 1) + part * LANES
                tables.append(weight * jnp.exp(-rate * (place + 1).astype(F32)))
            o_hi, o_lo = split(jnp.concatenate(tables, axis=1))
            table = jnp.concatenate([o_hi, o_hi, o_lo], axis=0)
            far = lax.dot_general(
                table, state, (((0,), (0,)), ((), ())), preferred_element_type=F32
            )
            base_ref[:, wide] = res_ref[:, wide].astype(F32) + query_ref[:, wide] * (
                ref[:, lanes] + far
            )

        return one

    each(first, make(0, fa_ref), 2)
    each(second, make(first, fb_ref), 2)


def chunks_of(groups):
    return [(c * groups // 8, (c + 1) * groups // 8) for c in range(8)]


def copy_out(source_ref, target_ref, sems, index, low, high):
    span = pl.ds(low * LANES, (high - low) * LANES)
    return pltpu.make_async_copy(source_ref.at[:, span], target_ref.at[:, span], sems.at[index])


def late_kernel(
    first,
    second,
    odd_ref,
    ta_ref,
    tb_ref,
    got_ref,
    near_ref,
    base_ref,
    query_ref,
    target_ref,
    out_ref,
    square_ref,
    sum_ref,
    sems,
):
    odd = odd_ref[0]
    sum_ref[...] = jnp.zeros_like(sum_ref)

    def finish(wide, term):
        rounded = (base_ref[:, wide] + query_ref[:, wide] * term).astype(BF16)
        out_ref[:, wide] = rounded
        back = rounded.astype(F32)
        sum_ref[...] += back * back

    def far(g):
        finish(at(g), dot(lag_two(ta_ref, g), got_ref[:, at(g)]))

    def merged(g):
        finish(at(g), got_ref[:, at(g)].astype(F32))

    def near(g):
        finish(at(g + first), dot(lag_one(tb_ref, g), near_ref[:, at(g)]))

    @pl.when(odd == 1)
    def _():
        each(first, far, 2)

    @pl.when(odd == 0)
    def _():
        each(first, merged, 2)

    copy_a = copy_out(out_ref, target_ref, sems, 0, 0, first)
    copy_a.start()
    each(second, near, 2)
    copy_b = copy_out(out_ref, target_ref, sems, 1, first, first + second)
    copy_b.start()
    turned = jnp.transpose(sum_ref[...])
    square_ref[...] = jnp.broadcast_to(jnp.sum(turned, axis=0, keepdims=True), square_ref.shape)
    copy_a.wait()
    copy_b.wait()


def norm_kernel(count, groups, total_ref, gain_ref, x_ref, target_ref, o_ref, sems):
    scale = jnp.transpose(lax.rsqrt(total_ref[...] * (1.0 / count) + 1e-05))
    wide = jnp.broadcast_to(scale[:, 0:1], (scale.shape[0], LANES))
    copies = []
    for index, (low, high) in enumerate(chunks_of(groups)):
        for g in range(low, high):
            lanes = at(g)
            o_ref[:, lanes] = (x_ref[:, lanes].astype(F32) * wide * gain_ref[:, lanes]).astype(BF16)
        copy = copy_out(o_ref, target_ref, sems, index, low, high)
        copy.start()
        copies.append(copy)
    for copy in copies:
        copy.wait()


def call(kernel, out_shape, name, *args, smem=0, scratch=(), loose=(), alias={}):
    specs = [pl.BlockSpec(memory_space=pltpu.SMEM)] * smem
    specs += [pl.BlockSpec(memory_space=pltpu.VMEM)] * (len(args) - smem)
    outs = [
        pl.BlockSpec(memory_space=pl.ANY if i in loose else pltpu.VMEM)
        for i in range(len(out_shape))
    ]
    return pl.pallas_call(
        kernel,
        in_specs=specs,
        out_specs=outs,
        out_shape=out_shape,
        scratch_shapes=scratch,
        input_output_aliases=alias,
        cost_estimate=pl.CostEstimate(flops=0, bytes_accessed=20000, transcendentals=0),
        compiler_params=pltpu.CompilerParams(vmem_limit_bytes=24 << 20),
        name=name,
    )(*args)


def body(
    query_proj,
    key_proj,
    value_proj,
    short_kernel,
    explicit_taps,
    decay_rate,
    residues,
    residual,
    norm_gain,
):
    length, channels = query_proj.shape
    groups, taps = explicit_taps.shape
    modes = decay_rate.shape[1]
    devices = lax.axis_size("ctx")
    first = groups // 2
    second = groups - first
    b_parts = ((second * 3) // 8, second - (second * 3) // 8)
    a_parts = ((first * 3) // 8, first - (first * 3) // 8)
    sizes = (*a_parts, *b_parts)
    wide_a = first * LANES
    wide_b = second * LANES
    odd = (lax.axis_index("ctx") % 2).astype(jnp.int32).reshape(1)
    is_odd = odd[0] == 1
    shape = jax.ShapeDtypeStruct

    last = pl.BlockSpec((16, channels), lambda s: (length // 16 - 1, 0))
    own_tail = pl.pallas_call(
        tail_kernel,
        grid=(1,),
        in_specs=[last, last, last],
        out_specs=pl.BlockSpec((8, channels), lambda s: (0, 0)),
        out_shape=shape((8, channels), BF16),
        name="tail",
    )(query_proj, key_proj, value_proj)
    tail = lax.ppermute(own_tail, "ctx", shifted_pairs(devices, 1))

    rate_t = decay_rate.T
    weight_t = (residues * jnp.sqrt(-jnp.expm1(-2.0 * decay_rate))).T
    flipped = jnp.flip(explicit_taps, axis=1).astype(F32)
    source = jnp.concatenate([flipped[:, taps - 1 :], flipped[:, : taps - 1]], axis=1)

    blocks = [shape((length, size * LANES), BF16) for size in sizes]
    mixed = call(
        lambda *refs: mix_kernel(sizes, *refs), blocks, "mix", key_proj, value_proj, short_kernel
    )
    xa1, xa2, xb1, xb2, window = call(
        lambda *refs: head_kernel(sizes, *refs),
        [*blocks, shape((modes, channels), F32)],
        "head",
        *mixed, key_proj, value_proj, tail, short_kernel, rate_t,
    )
    half = channels // 2
    mine = jnp.where(is_odd, window[:, half:], window[:, :half])
    beside = lax.ppermute(
        jnp.where(is_odd, window[:, :half], window[:, half:]), "ctx", swap_pairs(devices)
    )

    def tables(start, parts, x, source):
        count = sum(parts)
        return call(
            lambda *refs: table_kernel(start, parts, *refs),
            [shape((count, LANES, taps), BF16), shape((length, count * LANES), F32)],
            "table",
            source, rate_t, weight_t, *x,
        )

    wide_rate = jnp.broadcast_to(rate_t[:, :, None], (modes, groups, LANES)).reshape(modes, channels)
    wide_rate = jnp.where(is_odd, wide_rate[:, half:], wide_rate[:, :half])
    decay = lambda blocks: jnp.exp(-wide_rate * (length * blocks))

    ta, part_a = tables(0, a_parts, (xa1, xa2), source)
    beside = after(beside, part_a)
    pair = decay(1.0) * jnp.where(is_odd, beside, mine) + jnp.where(is_odd, mine, beside)
    far1 = lax.ppermute(xb1, "ctx", shifted_pairs(devices, 2))
    near1 = lax.ppermute(xa1, "ctx", swap_pairs(devices))
    got = lax.ppermute(pair, "ctx", shifted_pairs(devices, 2))
    tb, part_b = tables(first, b_parts, (xb1, xb2), after(source, pair))
    before = after(got, part_b)
    pair = pair + decay(2.0) * before
    far1, near1 = after(far1, part_b), after(near1, part_b)
    far2 = lax.ppermute(after(xb2, far1, near1, pair), "ctx", shifted_pairs(devices, 2))
    near2 = lax.ppermute(after(xa2, far1, near1, pair), "ctx", swap_pairs(devices))
    hop = 4
    while hop < devices:
        last = hop * 2 >= devices
        if last:
            far2, near2 = after(far2, pair), after(near2, pair)
        got = lax.ppermute(pair, "ctx", shifted_pairs(devices, hop))
        if last:
            send_a, send_b, keep_a = call(
                lambda *refs: merge_kernel(a_parts, b_parts, *refs),
                [
                    shape((length, wide_a), BF16),
                    shape((length, wide_b), BF16),
                    shape((length, wide_a), F32),
                ],
                "merge",
                odd, ta, near1, near2, xa1, xa2, part_a, far1, far2, xb1, xb2,
                smem=1,
            )
            got = after(got, keep_a)
        before = before + decay(float(hop - 2)) * got
        pair = pair + decay(float(hop)) * got
        hop *= 2
    onward = decay(1.0) * before + jnp.where(is_odd, beside, mine)
    other = lax.ppermute(
        after(jnp.where(is_odd, before, onward), keep_a), "ctx", swap_pairs(devices)
    )
    near_b = lax.ppermute(after(send_b, other), "ctx", swap_pairs(devices))
    got_a = lax.ppermute(send_a, "ctx", shifted_pairs(devices, 2))
    acc_b, query = call(
        lambda *refs: pre_kernel(first, *b_parts, *refs),
        [shape((length, wide_b), F32), shape((length, channels), F32)],
        "pre",
        tb, far1, far2, after(part_b, keep_a), query_proj, tail, short_kernel,
    )
    state = jnp.where(
        is_odd,
        jnp.concatenate([other, onward], axis=1),
        jnp.concatenate([before, other], axis=1),
    )
    (base,) = call(
        lambda *refs: state_kernel(first, second, *refs),
        [shape((length, channels), F32)],
        "state",
        keep_a, acc_b, state, rate_t, weight_t, query, residual,
    )
    block_out, again, squares = call(
        lambda *refs: late_kernel(first, second, *refs),
        [
            shape((length, channels), BF16),
            shape((length, channels), BF16),
            shape((8, length), F32),
        ],
        "late",
        odd, ta, tb, got_a, near_b, base, query,
        smem=1,
        scratch=[pltpu.VMEM((length, LANES), F32), pltpu.SemaphoreType.DMA((2,))],
        loose=(0,),
    )
    total = lax.psum(squares, "width")
    count = float(channels * lax.axis_size("width"))
    (normed,) = call(
        lambda *refs: norm_kernel(count, groups, *refs),
        [shape((length, channels), BF16)],
        "norm",
        total, norm_gain[None, :], again,
        scratch=[pltpu.VMEM((length, channels), BF16), pltpu.SemaphoreType.DMA((8,))],
        loose=(0,),
    )
    return (block_out, normed)


def solution(mesh):
    return jax.shard_map(
        body,
        mesh=mesh,
        in_specs=(
            P("ctx", "width"),
            P("ctx", "width"),
            P("ctx", "width"),
            P(None, None, "width"),
            P("width", None),
            P("width", None),
            P("width", None),
            P("ctx", "width"),
            P("width"),
        ),
        out_specs=(P("ctx", "width"), P("ctx", "width")),
        check_vma=False,
    )
```

```python
import jax
import jax.numpy as jnp
from jax import lax
from jax.experimental import pallas as pl
from jax.experimental.pallas import tpu as pltpu
from jax.sharding import PartitionSpec as P

F32 = jnp.float32
BF16 = jnp.bfloat16
LANES = 128


def shifted_pairs(length, by):
    return [(i, i + by) for i in range(length) if i + by < length]


def swap_pairs(length):
    return [(i, i ^ 1) for i in range(length)]


def dot(a, b):
    return jnp.dot(a, b, preferred_element_type=F32)


def split(x):
    hi = x.astype(BF16)
    return hi, (x - hi.astype(F32)).astype(BF16)


def each(count, body, unroll):
    def several(step, carry):
        for j in range(unroll):
            body(step * unroll + j)
        return carry

    lax.fori_loop(0, count // unroll, several, 0)
    for group in range(count - count % unroll, count):
        body(group)


def after(value, *others):
    return lax.optimization_barrier((value, *others))[0]


def at(group):
    if isinstance(group, int):
        return pl.ds(group * LANES, LANES)
    return pl.ds(pl.multiple_of(group * LANES, LANES), LANES)


def column(table, group):
    place = lax.broadcasted_iota(jnp.int32, table.shape, 1)
    picked = jnp.sum(jnp.where(place == group, table, 0.0), axis=1, keepdims=True)
    return jnp.broadcast_to(picked, (table.shape[0], LANES))


def taps_of(sk_ref, which, lanes):
    return [sk_ref[which, j : j + 1, lanes] for j in range(3)]


def tails_of(tail_ref, which, lanes):
    rows = tail_ref[0:8, lanes].astype(F32)
    return [rows[2 * which + j : 2 * which + j + 1] for j in range(2)]


def short_filter(ref, kern, lanes):
    rows = ref[:, lanes].astype(F32)
    return kern[0] * rows + kern[1] * pltpu.roll(rows, 1, 0) + kern[2] * pltpu.roll(rows, 2, 0)


def short_filter_top(ref, tail, kern, lanes):
    rows = ref[0:16, lanes].astype(F32)
    before, last = tail
    place = lax.broadcasted_iota(jnp.int32, rows.shape, 0)
    one = jnp.where(place == 0, last, pltpu.roll(rows, 1, 0))
    two = jnp.where(place == 0, before, jnp.where(place == 1, last, pltpu.roll(rows, 2, 0)))
    return kern[0] * rows + kern[1] * one + kern[2] * two


def tail_kernel(q_ref, k_ref, v_ref, o_ref):
    for which, ref in enumerate((q_ref, k_ref, v_ref)):
        o_ref[2 * which : 2 * which + 2, :] = ref[14:16, :]
    o_ref[6:8, :] = v_ref[14:16, :]


def mix_kernel(sizes, k_ref, v_ref, sk_ref, *x_refs):
    def make(start, x_ref):
        def one(g):
            source = at(g + start)
            x_ref[:, at(g)] = (
                short_filter(k_ref, taps_of(sk_ref, 1, source), source)
                * short_filter(v_ref, taps_of(sk_ref, 2, source), source)
            ).astype(BF16)

        return one

    start = 0
    for size, x_ref in zip(sizes, x_refs):
        each(size, make(start, x_ref), 2)
        start += size


def head_kernel(sizes, *refs):
    k_ref, v_ref, tail_ref, sk_ref, rate_ref, *x_refs, f_ref = refs[len(sizes) :]
    for source, x_ref in zip(refs, x_refs):
        x_ref[...] = source[...]
    length = k_ref.shape[0]

    def make(start, x_ref):
        def one(g):
            source = at(g + start)
            lanes = at(g)
            x_ref[0:16, lanes] = (
                short_filter_top(
                    k_ref, tails_of(tail_ref, 1, source), taps_of(sk_ref, 1, source), source
                )
                * short_filter_top(
                    v_ref, tails_of(tail_ref, 2, source), taps_of(sk_ref, 2, source), source
                )
            ).astype(BF16)
            rate = column(rate_ref[...], g + start)
            tables = []
            for part in range(length // LANES):
                place = lax.broadcasted_iota(jnp.int32, rate.shape, 1) + part * LANES
                tables.append(jnp.exp(-rate * (length - 1 - place).astype(F32)))
            hi, lo = split(jnp.concatenate(tables, axis=1))
            total = dot(jnp.concatenate([hi, lo], axis=0), x_ref[:, lanes])
            modes = rate.shape[0]
            f_ref[:, source] = total[:modes] + total[modes:]

        return one

    start = 0
    for size, x_ref in zip(sizes, x_refs):
        each(size, make(start, x_ref), 2)
        start += size


def table_kernel(start, pieces, source_ref, rate_ref, weight_ref, *refs):
    *x_refs, tb_ref, f_ref = refs
    done = 0
    for groups, x_ref in zip(pieces, x_refs):
        table_piece(start, done, groups, source_ref, rate_ref, weight_ref, x_ref, tb_ref, f_ref)
        done += groups


def table_piece(start, skip, groups, source_ref, rate_ref, weight_ref, x_ref, tb_ref, f_ref):
    taps = source_ref.shape[-1]
    row_at = lax.broadcasted_iota(jnp.int32, (LANES, LANES), 0)
    col_at = lax.broadcasted_iota(jnp.int32, (LANES, LANES), 1)
    below = col_at <= row_at
    place = lax.broadcasted_iota(jnp.int32, (1, LANES), 1)

    def one(g):
        lanes = at(g)
        taken = source_ref[pl.ds(g + start + skip, 1), :]
        band = pltpu.roll(jnp.broadcast_to(taken, (LANES, taps)), 0, 1, stride=1, stride_axis=0)
        tb_ref[g + skip, :, 0:LANES] = jnp.where(below, 0.0, band[:, 0:LANES]).astype(BF16)
        tb_ref[g + skip, :, LANES:] = band[:, LANES:].astype(BF16)
        rate = column(rate_ref[...], g + start + skip)
        weight = column(weight_ref[...], g + start + skip)

        def modal(lag):
            value = weight * jnp.exp(-rate * lag.astype(F32))
            return jnp.sum(value, axis=0, keepdims=True)

        first = taken[:, taps - LANES :] + modal(LANES - place)
        lag_zero = taken[:, 0:1] + modal(place * 0)[:, 0:1]
        second = taken[:, taps - 2 * LANES : taps - LANES] + modal(2 * LANES - place)
        second = jnp.where(place == 0, lag_zero, second)
        near = jnp.broadcast_to(jnp.concatenate([first, second], axis=1), (LANES, 2 * LANES))
        near = pltpu.roll(near, 0, 1, stride=1, stride_axis=0)
        zero_lag = jnp.where(below, near[:, LANES:], 0.0)
        low = jnp.concatenate([near[:, :LANES], zero_lag], axis=1)
        top = jnp.concatenate([zero_lag, jnp.zeros((LANES, LANES), F32)], axis=1)
        hi, lo = split(jnp.concatenate([top, low], axis=0))
        both = dot(jnp.concatenate([hi, lo], axis=0), x_ref[:, lanes])
        f_ref[:, at(g + skip)] = both[: 2 * LANES] + both[2 * LANES :]

    each(groups, one, 2)


def lag_one(tb_ref, g):
    return jnp.concatenate([tb_ref[g, :, 256:512], tb_ref[g, :, 128:384]], axis=0)


def lag_two(tb_ref, g):
    low = jnp.concatenate([jnp.zeros((LANES, LANES), BF16), tb_ref[g, :, 0:128]], axis=1)
    return jnp.concatenate([tb_ref[g, :, 0:256], low], axis=0)


def merge_kernel(
    a_parts,
    b_parts,
    odd_ref,
    tb_ref,
    near1_ref,
    near2_ref,
    own1_ref,
    own2_ref,
    f_ref,
    far1_ref,
    far2_ref,
    xb1_ref,
    xb2_ref,
    send_a_ref,
    send_b_ref,
    keep_ref,
):
    odd = odd_ref[0]
    edge = a_parts[0] * LANES
    middle = b_parts[0] * LANES

    @pl.when(odd == 1)
    def _():
        send_a_ref[:, :edge] = own1_ref[...]
        send_a_ref[:, edge:] = own2_ref[...]
        send_b_ref[:, :middle] = far1_ref[...]
        send_b_ref[:, middle:] = far2_ref[...]

        def make(skip, near_ref):
            def one(g):
                wide = at(g + skip)
                keep_ref[:, wide] = f_ref[:, wide] + dot(
                    lag_one(tb_ref, g + skip), near_ref[:, at(g)]
                )

            return one

        each(a_parts[0], make(0, near1_ref), 2)
        each(a_parts[1], make(a_parts[0], near2_ref), 2)

    @pl.when(odd == 0)
    def _():
        keep_ref[...] = f_ref[...]
        send_b_ref[:, :middle] = xb1_ref[...]
        send_b_ref[:, middle:] = xb2_ref[...]

        def make(skip, near_ref, own_ref):
            def one(g):
                send_a_ref[:, at(g + skip)] = (
                    dot(lag_one(tb_ref, g + skip), near_ref[:, at(g)])
                    + dot(lag_two(tb_ref, g + skip), own_ref[:, at(g)])
                ).astype(BF16)

            return one

        each(a_parts[0], make(0, near1_ref, own1_ref), 2)
        each(a_parts[1], make(a_parts[0], near2_ref, own2_ref), 2)


def pre_kernel(
    start, one, two, tb_ref, far1_ref, far2_ref, f_ref, q_ref, tail_ref, sk_ref, acc_ref, query_ref
):
    def filtered(g):
        lanes = at(g)
        kern = taps_of(sk_ref, 0, lanes)
        query_ref[:, lanes] = short_filter(q_ref, kern, lanes)
        query_ref[0:16, lanes] = short_filter_top(q_ref, tails_of(tail_ref, 0, lanes), kern, lanes)

    each(start, filtered, 2)

    def make(skip, far_ref):
        def added(g):
            lanes = at(g + skip)
            filtered(g + skip + start)
            acc_ref[:, lanes] = f_ref[:, lanes] + dot(lag_two(tb_ref, g + skip), far_ref[:, at(g)])

        return added

    each(one, make(0, far1_ref), 2)
    each(two, make(one, far2_ref), 2)


def state_kernel(
    first, second, fa_ref, fb_ref, state_ref, rate_ref, weight_ref, query_ref, res_ref, base_ref
):
    length = fa_ref.shape[0]

    def make(start, ref):
        def one(g):
            lanes = at(g)
            wide = at(g + start)
            rate = column(rate_ref[...], g + start)
            weight = column(weight_ref[...], g + start)
            s_hi, s_lo = split(state_ref[:, wide])
            state = jnp.concatenate([s_hi, s_lo, s_hi], axis=0)
            tables = []
            for part in range(length // LANES):
                place = lax.broadcasted_iota(jnp.int32, rate.shape, 1) + part * LANES
                tables.append(weight * jnp.exp(-rate * (place + 1).astype(F32)))
            o_hi, o_lo = split(jnp.concatenate(tables, axis=1))
            table = jnp.concatenate([o_hi, o_hi, o_lo], axis=0)
            far = lax.dot_general(
                table, state, (((0,), (0,)), ((), ())), preferred_element_type=F32
            )
            base_ref[:, wide] = res_ref[:, wide].astype(F32) + query_ref[:, wide] * (
                ref[:, lanes] + far
            )

        return one

    each(first, make(0, fa_ref), 2)
    each(second, make(first, fb_ref), 2)


def chunks_of(groups):
    return [(c * groups // 8, (c + 1) * groups // 8) for c in range(8)]


def copy_out(source_ref, target_ref, sems, index, low, high):
    span = pl.ds(low * LANES, (high - low) * LANES)
    return pltpu.make_async_copy(source_ref.at[:, span], target_ref.at[:, span], sems.at[index])


def finisher(start, base_ref, query_ref, out_ref, sum_ref):
    def finish(g, term):
        wide = at(g + start)
        rounded = (base_ref[:, wide] + query_ref[:, wide] * term).astype(BF16)
        out_ref[:, at(g)] = rounded
        back = rounded.astype(F32)
        sum_ref[...] += back * back

    return finish


def late_a_kernel(first, odd_ref, ta_ref, got_ref, base_ref, query_ref, out_ref, sum_ref):
    odd = odd_ref[0]
    sum_ref[...] = jnp.zeros_like(sum_ref)
    finish = finisher(0, base_ref, query_ref, out_ref, sum_ref)

    @pl.when(odd == 1)
    def _():
        each(first, lambda g: finish(g, dot(lag_two(ta_ref, g), got_ref[:, at(g)])), 2)

    @pl.when(odd == 0)
    def _():
        each(first, lambda g: finish(g, got_ref[:, at(g)].astype(F32)), 2)


def late_b_kernel(
    first,
    second,
    tb_ref,
    near_ref,
    base_ref,
    query_ref,
    out_a_ref,
    sum_a_ref,
    target_ref,
    out_ref,
    square_ref,
    sum_ref,
    sems,
):
    wide_a = first * LANES
    wide_b = second * LANES
    copy_a = pltpu.make_async_copy(out_a_ref, target_ref.at[:, pl.ds(0, wide_a)], sems.at[0])
    copy_a.start()
    sum_ref[...] = sum_a_ref[...]
    finish = finisher(first, base_ref, query_ref, out_ref, sum_ref)
    each(second, lambda g: finish(g, dot(lag_one(tb_ref, g), near_ref[:, at(g)])), 2)
    copy_b = pltpu.make_async_copy(out_ref, target_ref.at[:, pl.ds(wide_a, wide_b)], sems.at[1])
    copy_b.start()
    turned = jnp.transpose(sum_ref[...])
    square_ref[...] = jnp.broadcast_to(jnp.sum(turned, axis=0, keepdims=True), square_ref.shape)
    copy_a.wait()
    copy_b.wait()


def norm_kernel(
    count, first, second, total_ref, gain_ref, xa_ref, xb_ref, target_ref, o_ref, sems
):
    scale = jnp.transpose(lax.rsqrt(total_ref[...] * (1.0 / count) + 1e-05))
    wide = jnp.broadcast_to(scale[:, 0:1], (scale.shape[0], LANES))
    copies = []
    for index, (low, high) in enumerate(chunks_of(first + second)):
        for g in range(low, high):
            lanes = at(g)
            x = xa_ref[:, at(g)] if g < first else xb_ref[:, at(g - first)]
            o_ref[:, lanes] = (x.astype(F32) * wide * gain_ref[:, lanes]).astype(BF16)
        copy = copy_out(o_ref, target_ref, sems, index, low, high)
        copy.start()
        copies.append(copy)
    for copy in copies:
        copy.wait()


def call(kernel, out_shape, name, *args, smem=0, scratch=(), loose=(), alias={}):
    specs = [pl.BlockSpec(memory_space=pltpu.SMEM)] * smem
    specs += [pl.BlockSpec(memory_space=pltpu.VMEM)] * (len(args) - smem)
    outs = [
        pl.BlockSpec(memory_space=pl.ANY if i in loose else pltpu.VMEM)
        for i in range(len(out_shape))
    ]
    return pl.pallas_call(
        kernel,
        in_specs=specs,
        out_specs=outs,
        out_shape=out_shape,
        scratch_shapes=scratch,
        input_output_aliases=alias,
        cost_estimate=pl.CostEstimate(flops=0, bytes_accessed=20000, transcendentals=0),
        compiler_params=pltpu.CompilerParams(vmem_limit_bytes=24 << 20),
        name=name,
    )(*args)


def body(
    query_proj,
    key_proj,
    value_proj,
    short_kernel,
    explicit_taps,
    decay_rate,
    residues,
    residual,
    norm_gain,
):
    length, channels = query_proj.shape
    groups, taps = explicit_taps.shape
    modes = decay_rate.shape[1]
    devices = lax.axis_size("ctx")
    first = groups // 2
    second = groups - first
    b_parts = (second // 4, second - second // 4)
    a_parts = (first // 4, first - first // 4)
    sizes = (*a_parts, *b_parts)
    wide_a = first * LANES
    wide_b = second * LANES
    odd = (lax.axis_index("ctx") % 2).astype(jnp.int32).reshape(1)
    is_odd = odd[0] == 1
    shape = jax.ShapeDtypeStruct

    last = pl.BlockSpec((16, channels), lambda s: (length // 16 - 1, 0))
    own_tail = pl.pallas_call(
        tail_kernel,
        grid=(1,),
        in_specs=[last, last, last],
        out_specs=pl.BlockSpec((8, channels), lambda s: (0, 0)),
        out_shape=shape((8, channels), BF16),
        name="tail",
    )(query_proj, key_proj, value_proj)
    tail = lax.ppermute(own_tail, "ctx", shifted_pairs(devices, 1))

    rate_t = decay_rate.T
    weight_t = (residues * jnp.sqrt(-jnp.expm1(-2.0 * decay_rate))).T
    flipped = jnp.flip(explicit_taps, axis=1).astype(F32)
    source = jnp.concatenate([flipped[:, taps - 1 :], flipped[:, : taps - 1]], axis=1)

    blocks = [shape((length, size * LANES), BF16) for size in sizes]
    mixed = call(
        lambda *refs: mix_kernel(sizes, *refs), blocks, "mix", key_proj, value_proj, short_kernel
    )
    xa1, xa2, xb1, xb2, window = call(
        lambda *refs: head_kernel(sizes, *refs),
        [*blocks, shape((modes, channels), F32)],
        "head",
        *mixed, key_proj, value_proj, tail, short_kernel, rate_t,
    )
    half = channels // 2
    mine = jnp.where(is_odd, window[:, half:], window[:, :half])
    beside = lax.ppermute(
        jnp.where(is_odd, window[:, :half], window[:, half:]), "ctx", swap_pairs(devices)
    )

    def tables(start, parts, x, source):
        count = sum(parts)
        return call(
            lambda *refs: table_kernel(start, parts, *refs),
            [shape((count, LANES, taps), BF16), shape((length, count * LANES), F32)],
            "table",
            source, rate_t, weight_t, *x,
        )

    wide_rate = jnp.broadcast_to(rate_t[:, :, None], (modes, groups, LANES)).reshape(modes, channels)
    wide_rate = jnp.where(is_odd, wide_rate[:, half:], wide_rate[:, :half])
    decay = lambda blocks: jnp.exp(-wide_rate * (length * blocks))

    pair = decay(1.0) * jnp.where(is_odd, beside, mine) + jnp.where(is_odd, mine, beside)
    far1 = lax.ppermute(xb1, "ctx", shifted_pairs(devices, 2))
    near1 = lax.ppermute(xa1, "ctx", swap_pairs(devices))
    got = lax.ppermute(pair, "ctx", shifted_pairs(devices, 2))
    before = got
    pair = pair + decay(2.0) * before
    far2 = lax.ppermute(after(xb2, far1, near1, pair), "ctx", shifted_pairs(devices, 2))
    near2 = lax.ppermute(after(xa2, far1, near1, pair), "ctx", swap_pairs(devices))
    hop = 4
    while hop < devices:
        last = hop * 2 >= devices
        if last:
            ta, part_a = tables(0, a_parts, (xa1, xa2), after(source, pair))
            tb, part_b = tables(first, b_parts, (xb1, xb2), after(source, part_a))
            far2, near2 = after(far2, part_b), after(near2, part_b)
        got = lax.ppermute(pair, "ctx", shifted_pairs(devices, hop))
        if last:
            send_a, send_b, keep_a = call(
                lambda *refs: merge_kernel(a_parts, b_parts, *refs),
                [
                    shape((length, wide_a), BF16),
                    shape((length, wide_b), BF16),
                    shape((length, wide_a), F32),
                ],
                "merge",
                odd, ta, near1, near2, xa1, xa2, part_a, far1, far2, xb1, xb2,
                smem=1,
            )
            got = after(got, keep_a)
        before = before + decay(float(hop - 2)) * got
        pair = pair + decay(float(hop)) * got
        hop *= 2
    onward = decay(1.0) * before + jnp.where(is_odd, beside, mine)
    other = lax.ppermute(
        after(jnp.where(is_odd, before, onward), keep_a), "ctx", swap_pairs(devices)
    )
    near_b = lax.ppermute(after(send_b, other), "ctx", swap_pairs(devices))
    got_a = lax.ppermute(send_a, "ctx", shifted_pairs(devices, 2))
    acc_b, query = call(
        lambda *refs: pre_kernel(first, *b_parts, *refs),
        [shape((length, wide_b), F32), shape((length, channels), F32)],
        "pre",
        tb, far1, far2, after(part_b, keep_a), query_proj, tail, short_kernel,
    )
    state = jnp.where(
        is_odd,
        jnp.concatenate([other, onward], axis=1),
        jnp.concatenate([before, other], axis=1),
    )
    (base,) = call(
        lambda *refs: state_kernel(first, second, *refs),
        [shape((length, channels), F32)],
        "state",
        keep_a, acc_b, state, rate_t, weight_t, query, residual,
    )
    out_a, sum_a = call(
        lambda *refs: late_a_kernel(first, *refs),
        [shape((length, wide_a), BF16), shape((length, LANES), F32)],
        "late_a",
        odd, ta, got_a, base, query,
        smem=1,
    )
    block_out, out_b, squares = call(
        lambda *refs: late_b_kernel(first, second, *refs),
        [
            shape((length, channels), BF16),
            shape((length, wide_b), BF16),
            shape((8, length), F32),
        ],
        "late_b",
        tb, near_b, base, query, out_a, sum_a,
        scratch=[pltpu.VMEM((length, LANES), F32), pltpu.SemaphoreType.DMA((2,))],
        loose=(0,),
    )
    total = lax.psum(squares, "width")
    count = float(channels * lax.axis_size("width"))
    (normed,) = call(
        lambda *refs: norm_kernel(count, first, second, *refs),
        [shape((length, channels), BF16)],
        "norm",
        total, norm_gain[None, :], out_a, out_b,
        scratch=[pltpu.VMEM((length, channels), BF16), pltpu.SemaphoreType.DMA((8,))],
        loose=(0,),
    )
    return (block_out, normed)


def solution(mesh):
    return jax.shard_map(
        body,
        mesh=mesh,
        in_specs=(
            P("ctx", "width"),
            P("ctx", "width"),
            P("ctx", "width"),
            P(None, None, "width"),
            P("width", None),
            P("width", None),
            P("width", None),
            P("ctx", "width"),
            P("width"),
        ),
        out_specs=(P("ctx", "width"), P("ctx", "width")),
        check_vma=False,
    )
```

```python
import jax
import jax.numpy as jnp
from jax import lax
from jax.experimental import pallas as pl
from jax.experimental.pallas import tpu as pltpu
from jax.sharding import PartitionSpec as P

F32 = jnp.float32
BF16 = jnp.bfloat16
LANES = 128


def shifted_pairs(length, by):
    return [(i, i + by) for i in range(length) if i + by < length]


def swap_pairs(length):
    return [(i, i ^ 1) for i in range(length)]


def dot(a, b):
    return jnp.dot(a, b, preferred_element_type=F32)


def split(x):
    hi = x.astype(BF16)
    return hi, (x - hi.astype(F32)).astype(BF16)


def each(count, body, unroll):
    def several(step, carry):
        for j in range(unroll):
            body(step * unroll + j)
        return carry

    lax.fori_loop(0, count // unroll, several, 0)
    for group in range(count - count % unroll, count):
        body(group)


def after(value, *others):
    return lax.optimization_barrier((value, *others))[0]


def at(group):
    if isinstance(group, int):
        return pl.ds(group * LANES, LANES)
    return pl.ds(pl.multiple_of(group * LANES, LANES), LANES)


def column(table, group):
    place = lax.broadcasted_iota(jnp.int32, table.shape, 1)
    picked = jnp.sum(jnp.where(place == group, table, 0.0), axis=1, keepdims=True)
    return jnp.broadcast_to(picked, (table.shape[0], LANES))


def taps_of(sk_ref, which, lanes):
    return [sk_ref[which, j : j + 1, lanes] for j in range(3)]


def tails_of(tail_ref, which, lanes):
    rows = tail_ref[0:8, lanes].astype(F32)
    return [rows[2 * which + j : 2 * which + j + 1] for j in range(2)]


def short_filter(ref, kern, lanes):
    rows = ref[:, lanes].astype(F32)
    return kern[0] * rows + kern[1] * pltpu.roll(rows, 1, 0) + kern[2] * pltpu.roll(rows, 2, 0)


def short_filter_top(ref, tail, kern, lanes):
    rows = ref[0:16, lanes].astype(F32)
    before, last = tail
    place = lax.broadcasted_iota(jnp.int32, rows.shape, 0)
    one = jnp.where(place == 0, last, pltpu.roll(rows, 1, 0))
    two = jnp.where(place == 0, before, jnp.where(place == 1, last, pltpu.roll(rows, 2, 0)))
    return kern[0] * rows + kern[1] * one + kern[2] * two


def tail_kernel(q_ref, k_ref, v_ref, o_ref):
    for which, ref in enumerate((q_ref, k_ref, v_ref)):
        o_ref[2 * which : 2 * which + 2, :] = ref[14:16, :]
    o_ref[6:8, :] = v_ref[14:16, :]


def mix_kernel(sizes, k_ref, v_ref, sk_ref, *x_refs):
    def make(start, x_ref):
        def one(g):
            source = at(g + start)
            x_ref[:, at(g)] = (
                short_filter(k_ref, taps_of(sk_ref, 1, source), source)
                * short_filter(v_ref, taps_of(sk_ref, 2, source), source)
            ).astype(BF16)

        return one

    start = 0
    for size, x_ref in zip(sizes, x_refs):
        each(size, make(start, x_ref), 8)
        start += size


def head_kernel(sizes, *refs):
    k_ref, v_ref, tail_ref, sk_ref, rate_ref, *x_refs, f_ref = refs[len(sizes) :]
    for source, x_ref in zip(refs, x_refs):
        x_ref[...] = source[...]
    length = k_ref.shape[0]

    def make(start, x_ref):
        def one(g):
            source = at(g + start)
            lanes = at(g)
            x_ref[0:16, lanes] = (
                short_filter_top(
                    k_ref, tails_of(tail_ref, 1, source), taps_of(sk_ref, 1, source), source
                )
                * short_filter_top(
                    v_ref, tails_of(tail_ref, 2, source), taps_of(sk_ref, 2, source), source
                )
            ).astype(BF16)
            rate = column(rate_ref[...], g + start)
            tables = []
            for part in range(length // LANES):
                place = lax.broadcasted_iota(jnp.int32, rate.shape, 1) + part * LANES
                tables.append(jnp.exp(-rate * (length - 1 - place).astype(F32)))
            hi, lo = split(jnp.concatenate(tables, axis=1))
            total = dot(jnp.concatenate([hi, lo], axis=0), x_ref[:, lanes])
            modes = rate.shape[0]
            f_ref[:, source] = total[:modes] + total[modes:]

        return one

    start = 0
    for size, x_ref in zip(sizes, x_refs):
        each(size, make(start, x_ref), 8)
        start += size


def table_kernel(start, pieces, source_ref, rate_ref, weight_ref, *refs):
    *x_refs, tb_ref, f_ref = refs
    done = 0
    for groups, x_ref in zip(pieces, x_refs):
        table_piece(start, done, groups, source_ref, rate_ref, weight_ref, x_ref, tb_ref, f_ref)
        done += groups


def table_piece(start, skip, groups, source_ref, rate_ref, weight_ref, x_ref, tb_ref, f_ref):
    taps = source_ref.shape[-1]
    row_at = lax.broadcasted_iota(jnp.int32, (LANES, LANES), 0)
    col_at = lax.broadcasted_iota(jnp.int32, (LANES, LANES), 1)
    below = col_at <= row_at
    place = lax.broadcasted_iota(jnp.int32, (1, LANES), 1)

    def one(g):
        lanes = at(g)
        taken = source_ref[pl.ds(g + start + skip, 1), :]
        band = pltpu.roll(jnp.broadcast_to(taken, (LANES, taps)), 0, 1, stride=1, stride_axis=0)
        tb_ref[g + skip, :, 0:LANES] = jnp.where(below, 0.0, band[:, 0:LANES]).astype(BF16)
        tb_ref[g + skip, :, LANES:] = band[:, LANES:].astype(BF16)
        rate = column(rate_ref[...], g + start + skip)
        weight = column(weight_ref[...], g + start + skip)

        def modal(lag):
            value = weight * jnp.exp(-rate * lag.astype(F32))
            return jnp.sum(value, axis=0, keepdims=True)

        first = taken[:, taps - LANES :] + modal(LANES - place)
        lag_zero = taken[:, 0:1] + modal(place * 0)[:, 0:1]
        second = taken[:, taps - 2 * LANES : taps - LANES] + modal(2 * LANES - place)
        second = jnp.where(place == 0, lag_zero, second)
        near = jnp.broadcast_to(jnp.concatenate([first, second], axis=1), (LANES, 2 * LANES))
        near = pltpu.roll(near, 0, 1, stride=1, stride_axis=0)
        zero_lag = jnp.where(below, near[:, LANES:], 0.0)
        low = jnp.concatenate([near[:, :LANES], zero_lag], axis=1)
        top = jnp.concatenate([zero_lag, jnp.zeros((LANES, LANES), F32)], axis=1)
        hi, lo = split(jnp.concatenate([top, low], axis=0))
        both = dot(jnp.concatenate([hi, lo], axis=0), x_ref[:, lanes])
        f_ref[:, at(g + skip)] = both[: 2 * LANES] + both[2 * LANES :]

    each(groups, one, 4)


def lag_one(tb_ref, g):
    return jnp.concatenate([tb_ref[g, :, 256:512], tb_ref[g, :, 128:384]], axis=0)


def lag_two(tb_ref, g):
    low = jnp.concatenate([jnp.zeros((LANES, LANES), BF16), tb_ref[g, :, 0:128]], axis=1)
    return jnp.concatenate([tb_ref[g, :, 0:256], low], axis=0)


def merge_kernel(
    a_parts,
    b_parts,
    odd_ref,
    tb_ref,
    near1_ref,
    near2_ref,
    own1_ref,
    own2_ref,
    f_ref,
    far1_ref,
    far2_ref,
    xb1_ref,
    xb2_ref,
    send_a_ref,
    send_b_ref,
    keep_ref,
):
    odd = odd_ref[0]
    edge = a_parts[0] * LANES
    middle = b_parts[0] * LANES

    @pl.when(odd == 1)
    def _():
        send_a_ref[:, :edge] = own1_ref[...]
        send_a_ref[:, edge:] = own2_ref[...]
        send_b_ref[:, :middle] = far1_ref[...]
        send_b_ref[:, middle:] = far2_ref[...]

        def make(skip, near_ref):
            def one(g):
                wide = at(g + skip)
                keep_ref[:, wide] = f_ref[:, wide] + dot(
                    lag_one(tb_ref, g + skip), near_ref[:, at(g)]
                )

            return one

        each(a_parts[0], make(0, near1_ref), 8)
        each(a_parts[1], make(a_parts[0], near2_ref), 8)

    @pl.when(odd == 0)
    def _():
        keep_ref[...] = f_ref[...]
        send_b_ref[:, :middle] = xb1_ref[...]
        send_b_ref[:, middle:] = xb2_ref[...]

        def make(skip, near_ref, own_ref):
            def one(g):
                send_a_ref[:, at(g + skip)] = (
                    dot(lag_one(tb_ref, g + skip), near_ref[:, at(g)])
                    + dot(lag_two(tb_ref, g + skip), own_ref[:, at(g)])
                ).astype(BF16)

            return one

        each(a_parts[0], make(0, near1_ref, own1_ref), 8)
        each(a_parts[1], make(a_parts[0], near2_ref, own2_ref), 8)


def pre_kernel(
    start, one, two, tb_ref, far1_ref, far2_ref, f_ref, q_ref, tail_ref, sk_ref, acc_ref, query_ref
):
    def filtered(g):
        lanes = at(g)
        kern = taps_of(sk_ref, 0, lanes)
        query_ref[:, lanes] = short_filter(q_ref, kern, lanes)
        query_ref[0:16, lanes] = short_filter_top(q_ref, tails_of(tail_ref, 0, lanes), kern, lanes)

    each(start, filtered, 8)

    def make(skip, far_ref):
        def added(g):
            lanes = at(g + skip)
            filtered(g + skip + start)
            acc_ref[:, lanes] = f_ref[:, lanes] + dot(lag_two(tb_ref, g + skip), far_ref[:, at(g)])

        return added

    each(one, make(0, far1_ref), 8)
    each(two, make(one, far2_ref), 8)


def state_kernel(
    first, second, fa_ref, fb_ref, state_ref, rate_ref, weight_ref, query_ref, res_ref, base_ref
):
    length = fa_ref.shape[0]

    def make(start, ref):
        def one(g):
            lanes = at(g)
            wide = at(g + start)
            rate = column(rate_ref[...], g + start)
            weight = column(weight_ref[...], g + start)
            s_hi, s_lo = split(state_ref[:, wide])
            state = jnp.concatenate([s_hi, s_lo, s_hi], axis=0)
            tables = []
            for part in range(length // LANES):
                place = lax.broadcasted_iota(jnp.int32, rate.shape, 1) + part * LANES
                tables.append(weight * jnp.exp(-rate * (place + 1).astype(F32)))
            o_hi, o_lo = split(jnp.concatenate(tables, axis=1))
            table = jnp.concatenate([o_hi, o_hi, o_lo], axis=0)
            far = lax.dot_general(
                table, state, (((0,), (0,)), ((), ())), preferred_element_type=F32
            )
            base_ref[:, wide] = res_ref[:, wide].astype(F32) + query_ref[:, wide] * (
                ref[:, lanes] + far
            )

        return one

    each(first, make(0, fa_ref), 8)
    each(second, make(first, fb_ref), 8)


def chunks_of(groups):
    return [(c * groups // 8, (c + 1) * groups // 8) for c in range(8)]


def copy_out(source_ref, target_ref, sems, index, low, high):
    span = pl.ds(low * LANES, (high - low) * LANES)
    return pltpu.make_async_copy(source_ref.at[:, span], target_ref.at[:, span], sems.at[index])


def finisher(start, base_ref, query_ref, out_ref, sum_ref):
    def finish(g, term):
        wide = at(g + start)
        rounded = (base_ref[:, wide] + query_ref[:, wide] * term).astype(BF16)
        out_ref[:, at(g)] = rounded
        back = rounded.astype(F32)
        sum_ref[...] += back * back

    return finish


def late_a_kernel(first, odd_ref, ta_ref, got_ref, base_ref, query_ref, out_ref, sum_ref):
    odd = odd_ref[0]
    sum_ref[...] = jnp.zeros_like(sum_ref)
    finish = finisher(0, base_ref, query_ref, out_ref, sum_ref)

    @pl.when(odd == 1)
    def _():
        each(first, lambda g: finish(g, dot(lag_two(ta_ref, g), got_ref[:, at(g)])), 8)

    @pl.when(odd == 0)
    def _():
        each(first, lambda g: finish(g, got_ref[:, at(g)].astype(F32)), 8)


def late_b_kernel(
    first,
    second,
    tb_ref,
    near_ref,
    base_ref,
    query_ref,
    out_a_ref,
    sum_a_ref,
    target_ref,
    out_ref,
    square_ref,
    sum_ref,
    sems,
):
    wide_a = first * LANES
    wide_b = second * LANES
    copy_a = pltpu.make_async_copy(out_a_ref, target_ref.at[:, pl.ds(0, wide_a)], sems.at[0])
    copy_a.start()
    sum_ref[...] = sum_a_ref[...]
    finish = finisher(first, base_ref, query_ref, out_ref, sum_ref)
    each(second, lambda g: finish(g, dot(lag_one(tb_ref, g), near_ref[:, at(g)])), 8)
    copy_b = pltpu.make_async_copy(out_ref, target_ref.at[:, pl.ds(wide_a, wide_b)], sems.at[1])
    copy_b.start()
    turned = jnp.transpose(sum_ref[...])
    square_ref[...] = jnp.broadcast_to(jnp.sum(turned, axis=0, keepdims=True), square_ref.shape)
    copy_a.wait()
    copy_b.wait()


def norm_kernel(
    count, first, second, total_ref, gain_ref, xa_ref, xb_ref, target_ref, o_ref, sems
):
    scale = jnp.transpose(lax.rsqrt(total_ref[...] * (1.0 / count) + 1e-05))
    wide = jnp.broadcast_to(scale[:, 0:1], (scale.shape[0], LANES))
    copies = []
    for index, (low, high) in enumerate(chunks_of(first + second)):
        for g in range(low, high):
            lanes = at(g)
            x = xa_ref[:, at(g)] if g < first else xb_ref[:, at(g - first)]
            o_ref[:, lanes] = (x.astype(F32) * wide * gain_ref[:, lanes]).astype(BF16)
        copy = copy_out(o_ref, target_ref, sems, index, low, high)
        copy.start()
        copies.append(copy)
    for copy in copies:
        copy.wait()


def call(kernel, out_shape, name, *args, smem=0, scratch=(), loose=(), alias={}):
    specs = [pl.BlockSpec(memory_space=pltpu.SMEM)] * smem
    specs += [pl.BlockSpec(memory_space=pltpu.VMEM)] * (len(args) - smem)
    outs = [
        pl.BlockSpec(memory_space=pl.ANY if i in loose else pltpu.VMEM)
        for i in range(len(out_shape))
    ]
    return pl.pallas_call(
        kernel,
        in_specs=specs,
        out_specs=outs,
        out_shape=out_shape,
        scratch_shapes=scratch,
        input_output_aliases=alias,
        cost_estimate=pl.CostEstimate(flops=0, bytes_accessed=20000, transcendentals=0),
        compiler_params=pltpu.CompilerParams(vmem_limit_bytes=24 << 20),
        name=name,
    )(*args)


def body(
    query_proj,
    key_proj,
    value_proj,
    short_kernel,
    explicit_taps,
    decay_rate,
    residues,
    residual,
    norm_gain,
):
    length, channels = query_proj.shape
    groups, taps = explicit_taps.shape
    modes = decay_rate.shape[1]
    devices = lax.axis_size("ctx")
    first = groups // 2
    second = groups - first
    b_parts = (second // 4, second - second // 4)
    a_parts = (first // 4, first - first // 4)
    sizes = (*a_parts, *b_parts)
    wide_a = first * LANES
    wide_b = second * LANES
    odd = (lax.axis_index("ctx") % 2).astype(jnp.int32).reshape(1)
    is_odd = odd[0] == 1
    shape = jax.ShapeDtypeStruct

    last = pl.BlockSpec((16, channels), lambda s: (length // 16 - 1, 0))
    own_tail = pl.pallas_call(
        tail_kernel,
        grid=(1,),
        in_specs=[last, last, last],
        out_specs=pl.BlockSpec((8, channels), lambda s: (0, 0)),
        out_shape=shape((8, channels), BF16),
        name="tail",
    )(query_proj, key_proj, value_proj)
    tail = lax.ppermute(own_tail, "ctx", shifted_pairs(devices, 1))

    rate_t = decay_rate.T
    weight_t = (residues * jnp.sqrt(-jnp.expm1(-2.0 * decay_rate))).T
    flipped = jnp.flip(explicit_taps, axis=1).astype(F32)
    source = jnp.concatenate([flipped[:, taps - 1 :], flipped[:, : taps - 1]], axis=1)

    blocks = [shape((length, size * LANES), BF16) for size in sizes]
    mixed = call(
        lambda *refs: mix_kernel(sizes, *refs), blocks, "mix", key_proj, value_proj, short_kernel
    )
    xa1, xa2, xb1, xb2, window = call(
        lambda *refs: head_kernel(sizes, *refs),
        [*blocks, shape((modes, channels), F32)],
        "head",
        *mixed, key_proj, value_proj, tail, short_kernel, rate_t,
    )
    half = channels // 2
    mine = jnp.where(is_odd, window[:, half:], window[:, :half])
    beside = lax.ppermute(
        jnp.where(is_odd, window[:, :half], window[:, half:]), "ctx", swap_pairs(devices)
    )

    def tables(start, parts, x, source):
        count = sum(parts)
        return call(
            lambda *refs: table_kernel(start, parts, *refs),
            [shape((count, LANES, taps), BF16), shape((length, count * LANES), F32)],
            "table",
            source, rate_t, weight_t, *x,
        )

    wide_rate = jnp.broadcast_to(rate_t[:, :, None], (modes, groups, LANES)).reshape(modes, channels)
    wide_rate = jnp.where(is_odd, wide_rate[:, half:], wide_rate[:, :half])
    decay = lambda blocks: jnp.exp(-wide_rate * (length * blocks))

    pair = decay(1.0) * jnp.where(is_odd, beside, mine) + jnp.where(is_odd, mine, beside)
    far1 = lax.ppermute(xb1, "ctx", shifted_pairs(devices, 2))
    near1 = lax.ppermute(xa1, "ctx", swap_pairs(devices))
    got = lax.ppermute(pair, "ctx", shifted_pairs(devices, 2))
    before = got
    pair = pair + decay(2.0) * before
    far2 = lax.ppermute(after(xb2, far1, near1, pair), "ctx", shifted_pairs(devices, 2))
    near2 = lax.ppermute(after(xa2, far1, near1, pair), "ctx", swap_pairs(devices))
    hop = 4
    while hop < devices:
        last = hop * 2 >= devices
        if last:
            ta, part_a = tables(0, a_parts, (xa1, xa2), after(source, pair))
            tb, part_b = tables(first, b_parts, (xb1, xb2), after(source, part_a))
            far2, near2 = after(far2, part_b), after(near2, part_b)
        got = lax.ppermute(pair, "ctx", shifted_pairs(devices, hop))
        if last:
            send_a, send_b, keep_a = call(
                lambda *refs: merge_kernel(a_parts, b_parts, *refs),
                [
                    shape((length, wide_a), BF16),
                    shape((length, wide_b), BF16),
                    shape((length, wide_a), F32),
                ],
                "merge",
                odd, ta, near1, near2, xa1, xa2, part_a, far1, far2, xb1, xb2,
                smem=1,
            )
            got = after(got, keep_a)
        before = before + decay(float(hop - 2)) * got
        pair = pair + decay(float(hop)) * got
        hop *= 2
    onward = decay(1.0) * before + jnp.where(is_odd, beside, mine)
    other = lax.ppermute(
        after(jnp.where(is_odd, before, onward), keep_a), "ctx", swap_pairs(devices)
    )
    near_b = lax.ppermute(after(send_b, other), "ctx", swap_pairs(devices))
    got_a = lax.ppermute(send_a, "ctx", shifted_pairs(devices, 2))
    acc_b, query = call(
        lambda *refs: pre_kernel(first, *b_parts, *refs),
        [shape((length, wide_b), F32), shape((length, channels), F32)],
        "pre",
        tb, far1, far2, after(part_b, keep_a), query_proj, tail, short_kernel,
    )
    state = jnp.where(
        is_odd,
        jnp.concatenate([other, onward], axis=1),
        jnp.concatenate([before, other], axis=1),
    )
    (base,) = call(
        lambda *refs: state_kernel(first, second, *refs),
        [shape((length, channels), F32)],
        "state",
        keep_a, acc_b, state, rate_t, weight_t, query, residual,
    )
    out_a, sum_a = call(
        lambda *refs: late_a_kernel(first, *refs),
        [shape((length, wide_a), BF16), shape((length, LANES), F32)],
        "late_a",
        odd, ta, got_a, base, query,
        smem=1,
    )
    block_out, out_b, squares = call(
        lambda *refs: late_b_kernel(first, second, *refs),
        [
            shape((length, channels), BF16),
            shape((length, wide_b), BF16),
            shape((8, length), F32),
        ],
        "late_b",
        tb, near_b, base, query, out_a, sum_a,
        scratch=[pltpu.VMEM((length, LANES), F32), pltpu.SemaphoreType.DMA((2,))],
        loose=(0,),
    )
    total = lax.psum(squares, "width")
    count = float(channels * lax.axis_size("width"))
    (normed,) = call(
        lambda *refs: norm_kernel(count, first, second, *refs),
        [shape((length, channels), BF16)],
        "norm",
        total, norm_gain[None, :], out_a, out_b,
        scratch=[pltpu.VMEM((length, channels), BF16), pltpu.SemaphoreType.DMA((8,))],
        loose=(0,),
    )
    return (block_out, normed)


def solution(mesh):
    return jax.shard_map(
        body,
        mesh=mesh,
        in_specs=(
            P("ctx", "width"),
            P("ctx", "width"),
            P("ctx", "width"),
            P(None, None, "width"),
            P("width", None),
            P("width", None),
            P("width", None),
            P("ctx", "width"),
            P("width"),
        ),
        out_specs=(P("ctx", "width"), P("ctx", "width")),
        check_vma=False,
    )
```

```python
import jax
import jax.numpy as jnp
from jax import lax
from jax.experimental import pallas as pl
from jax.experimental.pallas import tpu as pltpu
from jax.sharding import PartitionSpec as P

F32 = jnp.float32
BF16 = jnp.bfloat16
LANES = 128


def shifted_pairs(length, by):
    return [(i, i + by) for i in range(length) if i + by < length]


def swap_pairs(length):
    return [(i, i ^ 1) for i in range(length)]


def dot(a, b):
    return jnp.dot(a, b, preferred_element_type=F32)


def split(x):
    hi = x.astype(BF16)
    return hi, (x - hi.astype(F32)).astype(BF16)


def each(count, body, unroll):
    def several(step, carry):
        for j in range(unroll):
            body(step * unroll + j)
        return carry

    lax.fori_loop(0, count // unroll, several, 0)
    for group in range(count - count % unroll, count):
        body(group)


def after(value, *others):
    return lax.optimization_barrier((value, *others))[0]


def at(group):
    if isinstance(group, int):
        return pl.ds(group * LANES, LANES)
    return pl.ds(pl.multiple_of(group * LANES, LANES), LANES)


def column(table, group):
    place = lax.broadcasted_iota(jnp.int32, table.shape, 1)
    picked = jnp.sum(jnp.where(place == group, table, 0.0), axis=1, keepdims=True)
    return jnp.broadcast_to(picked, (table.shape[0], LANES))


def taps_of(sk_ref, which, lanes):
    return [sk_ref[which, j : j + 1, lanes] for j in range(3)]


def tails_of(tail_ref, which, lanes):
    rows = tail_ref[0:8, lanes].astype(F32)
    return [rows[2 * which + j : 2 * which + j + 1] for j in range(2)]


def short_filter(ref, kern, lanes):
    rows = ref[:, lanes].astype(F32)
    return kern[0] * rows + kern[1] * pltpu.roll(rows, 1, 0) + kern[2] * pltpu.roll(rows, 2, 0)


def short_filter_top(ref, tail, kern, lanes):
    rows = ref[0:16, lanes].astype(F32)
    before, last = tail
    place = lax.broadcasted_iota(jnp.int32, rows.shape, 0)
    one = jnp.where(place == 0, last, pltpu.roll(rows, 1, 0))
    two = jnp.where(place == 0, before, jnp.where(place == 1, last, pltpu.roll(rows, 2, 0)))
    return kern[0] * rows + kern[1] * one + kern[2] * two


def tail_kernel(q_ref, k_ref, v_ref, o_ref):
    for which, ref in enumerate((q_ref, k_ref, v_ref)):
        o_ref[2 * which : 2 * which + 2, :] = ref[14:16, :]
    o_ref[6:8, :] = v_ref[14:16, :]


def mix_kernel(sizes, k_ref, v_ref, sk_ref, *x_refs):
    def make(start, x_ref):
        def one(g):
            source = at(g + start)
            x_ref[:, at(g)] = (
                short_filter(k_ref, taps_of(sk_ref, 1, source), source)
                * short_filter(v_ref, taps_of(sk_ref, 2, source), source)
            ).astype(BF16)

        return one

    start = 0
    for size, x_ref in zip(sizes, x_refs):
        each(size, make(start, x_ref), 8)
        start += size


def head_kernel(sizes, *refs):
    k_ref, v_ref, tail_ref, sk_ref, rate_ref, *x_refs, f_ref = refs[len(sizes) :]
    for source, x_ref in zip(refs, x_refs):
        x_ref[...] = source[...]
    length = k_ref.shape[0]

    def make(start, x_ref):
        def one(g):
            source = at(g + start)
            lanes = at(g)
            x_ref[0:16, lanes] = (
                short_filter_top(
                    k_ref, tails_of(tail_ref, 1, source), taps_of(sk_ref, 1, source), source
                )
                * short_filter_top(
                    v_ref, tails_of(tail_ref, 2, source), taps_of(sk_ref, 2, source), source
                )
            ).astype(BF16)
            rate = column(rate_ref[...], g + start)
            tables = []
            for part in range(length // LANES):
                place = lax.broadcasted_iota(jnp.int32, rate.shape, 1) + part * LANES
                tables.append(jnp.exp(-rate * (length - 1 - place).astype(F32)))
            hi, lo = split(jnp.concatenate(tables, axis=1))
            total = dot(jnp.concatenate([hi, lo], axis=0), x_ref[:, lanes])
            modes = rate.shape[0]
            f_ref[:, source] = total[:modes] + total[modes:]

        return one

    start = 0
    for size, x_ref in zip(sizes, x_refs):
        each(size, make(start, x_ref), 8)
        start += size


def table_kernel(start, pieces, source_ref, rate_ref, weight_ref, *refs):
    *x_refs, tb_ref, f_ref = refs
    done = 0
    for groups, x_ref in zip(pieces, x_refs):
        table_piece(start, done, groups, source_ref, rate_ref, weight_ref, x_ref, tb_ref, f_ref)
        done += groups


def table_piece(start, skip, groups, source_ref, rate_ref, weight_ref, x_ref, tb_ref, f_ref):
    taps = source_ref.shape[-1]
    row_at = lax.broadcasted_iota(jnp.int32, (LANES, LANES), 0)
    col_at = lax.broadcasted_iota(jnp.int32, (LANES, LANES), 1)
    below = col_at <= row_at
    place = lax.broadcasted_iota(jnp.int32, (1, LANES), 1)

    def one(g):
        lanes = at(g)
        taken = source_ref[pl.ds(g + start + skip, 1), :]
        band = pltpu.roll(jnp.broadcast_to(taken, (LANES, taps)), 0, 1, stride=1, stride_axis=0)
        tb_ref[g + skip, :, 0:LANES] = jnp.where(below, 0.0, band[:, 0:LANES]).astype(BF16)
        tb_ref[g + skip, :, LANES:] = band[:, LANES:].astype(BF16)
        rate = column(rate_ref[...], g + start + skip)
        weight = column(weight_ref[...], g + start + skip)

        def modal(lag):
            value = weight * jnp.exp(-rate * lag.astype(F32))
            return jnp.sum(value, axis=0, keepdims=True)

        first = taken[:, taps - LANES :] + modal(LANES - place)
        lag_zero = taken[:, 0:1] + modal(place * 0)[:, 0:1]
        second = taken[:, taps - 2 * LANES : taps - LANES] + modal(2 * LANES - place)
        second = jnp.where(place == 0, lag_zero, second)
        near = jnp.broadcast_to(jnp.concatenate([first, second], axis=1), (LANES, 2 * LANES))
        near = pltpu.roll(near, 0, 1, stride=1, stride_axis=0)
        zero_lag = jnp.where(below, near[:, LANES:], 0.0)
        low = jnp.concatenate([near[:, :LANES], zero_lag], axis=1)
        top = jnp.concatenate([zero_lag, jnp.zeros((LANES, LANES), F32)], axis=1)
        hi, lo = split(jnp.concatenate([top, low], axis=0))
        both = dot(jnp.concatenate([hi, lo], axis=0), x_ref[:, lanes])
        f_ref[:, at(g + skip)] = both[: 2 * LANES] + both[2 * LANES :]

    each(groups, one, 4)


def lag_one(tb_ref, g):
    return jnp.concatenate([tb_ref[g, :, 256:512], tb_ref[g, :, 128:384]], axis=0)


def lag_two(tb_ref, g):
    low = jnp.concatenate([jnp.zeros((LANES, LANES), BF16), tb_ref[g, :, 0:128]], axis=1)
    return jnp.concatenate([tb_ref[g, :, 0:256], low], axis=0)


def merge_kernel(
    a_parts,
    b_parts,
    odd_ref,
    tb_ref,
    near1_ref,
    near2_ref,
    own1_ref,
    own2_ref,
    f_ref,
    far1_ref,
    far2_ref,
    xb1_ref,
    xb2_ref,
    send_a_ref,
    send_b_ref,
    keep_ref,
):
    odd = odd_ref[0]
    edge = a_parts[0] * LANES
    middle = b_parts[0] * LANES

    @pl.when(odd == 1)
    def _():
        send_a_ref[:, :edge] = own1_ref[...]
        send_a_ref[:, edge:] = own2_ref[...]
        send_b_ref[:, :middle] = far1_ref[...]
        send_b_ref[:, middle:] = far2_ref[...]

        def make(skip, near_ref):
            def one(g):
                wide = at(g + skip)
                keep_ref[:, wide] = f_ref[:, wide] + dot(
                    lag_one(tb_ref, g + skip), near_ref[:, at(g)]
                )

            return one

        each(a_parts[0], make(0, near1_ref), 8)
        each(a_parts[1], make(a_parts[0], near2_ref), 8)

    @pl.when(odd == 0)
    def _():
        keep_ref[...] = f_ref[...]
        send_b_ref[:, :middle] = xb1_ref[...]
        send_b_ref[:, middle:] = xb2_ref[...]

        def make(skip, near_ref, own_ref):
            def one(g):
                send_a_ref[:, at(g + skip)] = (
                    dot(lag_one(tb_ref, g + skip), near_ref[:, at(g)])
                    + dot(lag_two(tb_ref, g + skip), own_ref[:, at(g)])
                ).astype(BF16)

            return one

        each(a_parts[0], make(0, near1_ref, own1_ref), 8)
        each(a_parts[1], make(a_parts[0], near2_ref, own2_ref), 8)


def pre_kernel(
    start, one, two, tb_ref, far1_ref, far2_ref, f_ref, q_ref, tail_ref, sk_ref, acc_ref, query_ref
):
    def filtered(g):
        lanes = at(g)
        kern = taps_of(sk_ref, 0, lanes)
        query_ref[:, lanes] = short_filter(q_ref, kern, lanes)
        query_ref[0:16, lanes] = short_filter_top(q_ref, tails_of(tail_ref, 0, lanes), kern, lanes)

    each(start, filtered, 8)

    def make(skip, far_ref):
        def added(g):
            lanes = at(g + skip)
            filtered(g + skip + start)
            acc_ref[:, lanes] = f_ref[:, lanes] + dot(lag_two(tb_ref, g + skip), far_ref[:, at(g)])

        return added

    each(one, make(0, far1_ref), 8)
    each(two, make(one, far2_ref), 8)


def state_kernel(
    first, second, fa_ref, fb_ref, state_ref, rate_ref, weight_ref, query_ref, res_ref, base_ref
):
    length = fa_ref.shape[0]

    def make(start, ref):
        def one(g):
            lanes = at(g)
            wide = at(g + start)
            rate = column(rate_ref[...], g + start)
            weight = column(weight_ref[...], g + start)
            s_hi, s_lo = split(state_ref[:, wide])
            state = jnp.concatenate([s_hi, s_lo, s_hi], axis=0)
            tables = []
            for part in range(length // LANES):
                place = lax.broadcasted_iota(jnp.int32, rate.shape, 1) + part * LANES
                tables.append(weight * jnp.exp(-rate * (place + 1).astype(F32)))
            o_hi, o_lo = split(jnp.concatenate(tables, axis=1))
            table = jnp.concatenate([o_hi, o_hi, o_lo], axis=0)
            far = lax.dot_general(
                table, state, (((0,), (0,)), ((), ())), preferred_element_type=F32
            )
            base_ref[:, wide] = res_ref[:, wide].astype(F32) + query_ref[:, wide] * (
                ref[:, lanes] + far
            )

        return one

    each(first, make(0, fa_ref), 8)
    each(second, make(first, fb_ref), 8)


def chunks_of(groups):
    return [(c * groups // 8, (c + 1) * groups // 8) for c in range(8)]


def copy_out(source_ref, target_ref, sems, index, low, high):
    span = pl.ds(low * LANES, (high - low) * LANES)
    return pltpu.make_async_copy(source_ref.at[:, span], target_ref.at[:, span], sems.at[index])


def finisher(start, base_ref, query_ref, out_ref, sum_ref):
    def finish(g, term):
        wide = at(g + start)
        rounded = (base_ref[:, wide] + query_ref[:, wide] * term).astype(BF16)
        out_ref[:, at(g)] = rounded
        back = rounded.astype(F32)
        sum_ref[...] += back * back

    return finish


def late_a_kernel(first, odd_ref, ta_ref, got_ref, base_ref, query_ref, out_ref, sum_ref):
    odd = odd_ref[0]
    sum_ref[...] = jnp.zeros_like(sum_ref)
    finish = finisher(0, base_ref, query_ref, out_ref, sum_ref)

    @pl.when(odd == 1)
    def _():
        each(first, lambda g: finish(g, dot(lag_two(ta_ref, g), got_ref[:, at(g)])), 8)

    @pl.when(odd == 0)
    def _():
        each(first, lambda g: finish(g, got_ref[:, at(g)].astype(F32)), 8)


def late_b_kernel(
    first,
    second,
    tb_ref,
    near_ref,
    base_ref,
    query_ref,
    out_a_ref,
    sum_a_ref,
    target_ref,
    out_ref,
    square_ref,
    sum_ref,
    sems,
):
    wide_a = first * LANES
    wide_b = second * LANES
    copy_a = pltpu.make_async_copy(out_a_ref, target_ref.at[:, pl.ds(0, wide_a)], sems.at[0])
    copy_a.start()
    sum_ref[...] = sum_a_ref[...]
    finish = finisher(first, base_ref, query_ref, out_ref, sum_ref)
    each(second, lambda g: finish(g, dot(lag_one(tb_ref, g), near_ref[:, at(g)])), 8)
    copy_b = pltpu.make_async_copy(out_ref, target_ref.at[:, pl.ds(wide_a, wide_b)], sems.at[1])
    copy_b.start()
    turned = jnp.transpose(sum_ref[...])
    square_ref[...] = jnp.broadcast_to(jnp.sum(turned, axis=0, keepdims=True), square_ref.shape)
    copy_a.wait()
    copy_b.wait()


def norm_kernel(
    count, first, second, total_ref, gain_ref, xa_ref, xb_ref, target_ref, o_ref, sems
):
    scale = jnp.transpose(lax.rsqrt(total_ref[...] * (1.0 / count) + 1e-05))
    wide = jnp.broadcast_to(scale[:, 0:1], (scale.shape[0], LANES))
    copies = []
    for index, (low, high) in enumerate(chunks_of(first + second)):
        for g in range(low, high):
            lanes = at(g)
            x = xa_ref[:, at(g)] if g < first else xb_ref[:, at(g - first)]
            o_ref[:, lanes] = (x.astype(F32) * wide * gain_ref[:, lanes]).astype(BF16)
        copy = copy_out(o_ref, target_ref, sems, index, low, high)
        copy.start()
        copies.append(copy)
    for copy in copies:
        copy.wait()


def call(kernel, out_shape, name, *args, smem=0, scratch=(), loose=(), alias={}):
    specs = [pl.BlockSpec(memory_space=pltpu.SMEM)] * smem
    specs += [pl.BlockSpec(memory_space=pltpu.VMEM)] * (len(args) - smem)
    outs = [
        pl.BlockSpec(memory_space=pl.ANY if i in loose else pltpu.VMEM)
        for i in range(len(out_shape))
    ]
    return pl.pallas_call(
        kernel,
        in_specs=specs,
        out_specs=outs,
        out_shape=out_shape,
        scratch_shapes=scratch,
        input_output_aliases=alias,
        cost_estimate=pl.CostEstimate(flops=0, bytes_accessed=20000, transcendentals=0),
        compiler_params=pltpu.CompilerParams(vmem_limit_bytes=24 << 20),
        name=name,
    )(*args)


def body(
    query_proj,
    key_proj,
    value_proj,
    short_kernel,
    explicit_taps,
    decay_rate,
    residues,
    residual,
    norm_gain,
):
    length, channels = query_proj.shape
    groups, taps = explicit_taps.shape
    modes = decay_rate.shape[1]
    devices = lax.axis_size("ctx")
    first = groups // 2
    second = groups - first
    b_parts = (second // 4, second - second // 4)
    a_parts = (first // 4, first - first // 4)
    sizes = (*a_parts, *b_parts)
    wide_a = first * LANES
    wide_b = second * LANES
    odd = (lax.axis_index("ctx") % 2).astype(jnp.int32).reshape(1)
    is_odd = odd[0] == 1
    shape = jax.ShapeDtypeStruct

    last = pl.BlockSpec((16, channels), lambda s: (length // 16 - 1, 0))
    own_tail = pl.pallas_call(
        tail_kernel,
        grid=(1,),
        in_specs=[last, last, last],
        out_specs=pl.BlockSpec((8, channels), lambda s: (0, 0)),
        out_shape=shape((8, channels), BF16),
        name="tail",
    )(query_proj, key_proj, value_proj)
    tail = lax.ppermute(own_tail, "ctx", shifted_pairs(devices, 1))

    rate_t = decay_rate.T
    weight_t = (residues * jnp.sqrt(-jnp.expm1(-2.0 * decay_rate))).T
    flipped = jnp.flip(explicit_taps, axis=1).astype(F32)
    source = jnp.concatenate([flipped[:, taps - 1 :], flipped[:, : taps - 1]], axis=1)

    blocks = [shape((length, size * LANES), BF16) for size in sizes]
    mixed = call(
        lambda *refs: mix_kernel(sizes, *refs), blocks, "mix", key_proj, value_proj, short_kernel
    )
    xa1, xa2, xb1, xb2, window = call(
        lambda *refs: head_kernel(sizes, *refs),
        [*blocks, shape((modes, channels), F32)],
        "head",
        *mixed, key_proj, value_proj, tail, short_kernel, rate_t,
    )
    half = channels // 2
    mine = jnp.where(is_odd, window[:, half:], window[:, :half])
    beside = lax.ppermute(
        jnp.where(is_odd, window[:, :half], window[:, half:]), "ctx", swap_pairs(devices)
    )

    def tables(start, parts, x, source):
        count = sum(parts)
        return call(
            lambda *refs: table_kernel(start, parts, *refs),
            [shape((count, LANES, taps), BF16), shape((length, count * LANES), F32)],
            "table",
            source, rate_t, weight_t, *x,
        )

    wide_rate = jnp.broadcast_to(rate_t[:, :, None], (modes, groups, LANES)).reshape(modes, channels)
    wide_rate = jnp.where(is_odd, wide_rate[:, half:], wide_rate[:, :half])
    decay = lambda blocks: jnp.exp(-wide_rate * (length * blocks))

    pair = decay(1.0) * jnp.where(is_odd, beside, mine) + jnp.where(is_odd, mine, beside)
    far1 = lax.ppermute(xb1, "ctx", shifted_pairs(devices, 2))
    near1 = lax.ppermute(xa1, "ctx", swap_pairs(devices))
    got = lax.ppermute(pair, "ctx", shifted_pairs(devices, 2))
    before = got
    pair = pair + decay(2.0) * before
    far2 = lax.ppermute(after(xb2, far1, pair), "ctx", shifted_pairs(devices, 2))
    near2 = lax.ppermute(after(xa2, near1, pair), "ctx", swap_pairs(devices))
    hop = 4
    while hop < devices:
        last = hop * 2 >= devices
        if last:
            ta, part_a = tables(0, a_parts, (xa1, xa2), after(source, pair))
            tb, part_b = tables(first, b_parts, (xb1, xb2), after(source, part_a))
            far2, near2 = after(far2, part_b), after(near2, part_b)
        got = lax.ppermute(pair, "ctx", shifted_pairs(devices, hop))
        if last:
            send_a, send_b, keep_a = call(
                lambda *refs: merge_kernel(a_parts, b_parts, *refs),
                [
                    shape((length, wide_a), BF16),
                    shape((length, wide_b), BF16),
                    shape((length, wide_a), F32),
                ],
                "merge",
                odd, ta, near1, near2, xa1, xa2, part_a, far1, far2, xb1, xb2,
                smem=1,
            )
            got = after(got, keep_a)
        before = before + decay(float(hop - 2)) * got
        pair = pair + decay(float(hop)) * got
        hop *= 2
    onward = decay(1.0) * before + jnp.where(is_odd, beside, mine)
    other = lax.ppermute(
        after(jnp.where(is_odd, before, onward), keep_a), "ctx", swap_pairs(devices)
    )
    near_b = lax.ppermute(after(send_b, other), "ctx", swap_pairs(devices))
    got_a = lax.ppermute(send_a, "ctx", shifted_pairs(devices, 2))
    acc_b, query = call(
        lambda *refs: pre_kernel(first, *b_parts, *refs),
        [shape((length, wide_b), F32), shape((length, channels), F32)],
        "pre",
        tb, far1, far2, after(part_b, keep_a), query_proj, tail, short_kernel,
    )
    state = jnp.where(
        is_odd,
        jnp.concatenate([other, onward], axis=1),
        jnp.concatenate([before, other], axis=1),
    )
    (base,) = call(
        lambda *refs: state_kernel(first, second, *refs),
        [shape((length, channels), F32)],
        "state",
        keep_a, acc_b, state, rate_t, weight_t, query, residual,
    )
    out_a, sum_a = call(
        lambda *refs: late_a_kernel(first, *refs),
        [shape((length, wide_a), BF16), shape((length, LANES), F32)],
        "late_a",
        odd, ta, got_a, base, query,
        smem=1,
    )
    block_out, out_b, squares = call(
        lambda *refs: late_b_kernel(first, second, *refs),
        [
            shape((length, channels), BF16),
            shape((length, wide_b), BF16),
            shape((8, length), F32),
        ],
        "late_b",
        tb, near_b, base, query, out_a, sum_a,
        scratch=[pltpu.VMEM((length, LANES), F32), pltpu.SemaphoreType.DMA((2,))],
        loose=(0,),
    )
    total = lax.psum(squares, "width")
    count = float(channels * lax.axis_size("width"))
    (normed,) = call(
        lambda *refs: norm_kernel(count, first, second, *refs),
        [shape((length, channels), BF16)],
        "norm",
        total, norm_gain[None, :], out_a, out_b,
        scratch=[pltpu.VMEM((length, channels), BF16), pltpu.SemaphoreType.DMA((8,))],
        loose=(0,),
    )
    return (block_out, normed)


def solution(mesh):
    return jax.shard_map(
        body,
        mesh=mesh,
        in_specs=(
            P("ctx", "width"),
            P("ctx", "width"),
            P("ctx", "width"),
            P(None, None, "width"),
            P("width", None),
            P("width", None),
            P("width", None),
            P("ctx", "width"),
            P("width"),
        ),
        out_specs=(P("ctx", "width"), P("ctx", "width")),
        check_vma=False,
    )
```
